32 devices in a mesh: branch: 2 (over x), strip: 16 (over z, y, core).
Axes of the slice: x: 2, y: 2, z: 4, core: 2. Of those that a mesh axis runs over, the one named last changes fastest.
Arguments:
- image_feats: bfloat16 [32, 2048, 256], P(None, ('branch', 'strip')), may hold values from -6 to 6
- cam_weights: bfloat16 [3, 9, 256, 256], replicated, may hold values from -0.1875 to 0.1875
- depth_weight: bfloat16 [256, 118], replicated, may hold values from -1.5 to 1.5
- ray_bins: int32 [2048, 118], P(('branch', 'strip')), may hold values from 0 to 2047, as said below
- pillar_sums: bfloat16 [32, 256, 128], P(None, ('branch', 'strip')), may hold values from -12 to 12
- pillar_counts: int32 [32, 256], P(None, ('branch', 'strip')), may hold values from 0 to 8
- lidar_weight: bfloat16 [4, 128, 128], replicated, may hold values from -0.375 to 0.375
- merge_weight: bfloat16 [9, 384, 256], replicated, may hold values from -0.15625 to 0.15625
- out_cotangent: bfloat16 [16, 128, 256], P(None, ('branch', 'strip')), may hold values from -6 to 6
Outputs:
- merged: bfloat16 [16, 128, 256], P(None, ('branch', 'strip'))
- cam_grad: bfloat16 [32, 2048, 256], P(None, ('branch', 'strip'))
- lid_grad: bfloat16 [16, 128, 128], P(None, ('branch', 'strip'))
The draws below stay inside these ranges and needn't reach their ends.
Inputs may be any that keep to these rules, and one draw needn't show every extreme that they name: For a column j of sector s = j // 64, ray_bins[j, k] lies in sector s - 1, s or s + 1 taken modulo 32, in cycle k * 16 // 118.
All inputs are finite; a program needn't handle non-finite values.
Results may differ from the reference program's by a relative error of at most 0.014.
Values may be sent and summed in bfloat16 or wider, within the bound.
A program may use at most 128 MiB of HBM per device.

```python
import jax
import jax.numpy as jnp
from jax import lax

C = 256
CL = 128
CF = 256
DB = 118
ROWS = 32
LAYERS = 3
COLS_DEV = 64
BR = 16
BA = 4
NSECT = 32
NCOL = 2048
NA = 128
BCELL = 64
CC = 384


def draw_ray_bins(key, part):
    first_key, second_key = jax.random.split(jax.random.fold_in(key, 17))
    col_sector = (jnp.arange(NCOL, dtype=jnp.int32) // COLS_DEV)[:, None]
    steps = jax.random.randint(first_key, (NCOL, DB), -1, 2).astype(jnp.int32)
    slots = jax.random.randint(second_key, (NCOL, DB), 0, BA).astype(jnp.int32)
    cycles = (jnp.arange(DB, dtype=jnp.int32) * BR // DB)[None, :]
    sectors = (col_sector + steps) % NSECT
    return (sectors * (BR * BA) + cycles * BA + slots).astype(jnp.int32)


def plant(values, key, low, high):
    place = [jax.random.randint(jax.random.fold_in(key, axis), (), 0, length) for axis, length in enumerate(values.shape)]
    main_axis = values.shape.index(max(values.shape))
    neighbour = place[:main_axis] + [(place[main_axis] + 1) % values.shape[main_axis]] + place[main_axis + 1:]
    return values.at[tuple(place)].set(low).at[tuple(neighbour)].set(high)


def levels(stream_key, shape, cuts, smallest, largest):
    factor_of, own = 1.0, jax.random.fold_in(stream_key, 6)
    for axis_at, blocks in cuts:
        draws = jnp.exp(jax.random.uniform(jax.random.fold_in(own, axis_at), (blocks,), jnp.float32, smallest / len(cuts), largest / len(cuts)))
        factor_of = factor_of * jnp.repeat(draws, shape[axis_at] // blocks).reshape([-1 if axis == axis_at else 1 for axis in range(len(shape))])
    return factor_of


def gaussian(own_key, shape, scale, reach, pieces=(), held_as=jnp.bfloat16):
    array = scale * jax.random.normal(own_key, shape, jnp.float32)
    if pieces:
        array = array * levels(own_key, shape, pieces, -0.22, 0.18)
    return jnp.clip(array, -reach, reach).astype(held_as)


def setup_inputs(seed: int = 0) -> dict:
    key_of = jax.random.split(jax.random.key(seed), 10)
    return {
        "image_feats": gaussian(key_of[0], (ROWS, NCOL, C), 1.0, 6.0, ((1, 32),)),
        "cam_weights": gaussian(key_of[1], (LAYERS, 9, C, C), (9 * C // 2) ** -0.5, 0.1875),
        "depth_weight": gaussian(key_of[2], (C, DB), (C // 16) ** -0.5, 1.5),
        "ray_bins": draw_ray_bins(jax.random.fold_in(key_of[9], 71), 0),
        "pillar_sums": gaussian(key_of[4], (2 * BR, 2 * NA, CL), 2.0, 12.0, ((1, 32),)),
        "pillar_counts": plant(jax.random.randint(key_of[5], (2 * BR, 2 * NA), 0, 9), jax.random.fold_in(key_of[5], 1), 0, 8).astype(jnp.int32),
        "lidar_weight": gaussian(key_of[6], (4, CL, CL), (2 * CL) ** -0.5, 0.375),
        "merge_weight": gaussian(key_of[7], (9, CC, CF), (9 * CC // 2) ** -0.5, 0.15625),
        "out_cotangent": gaussian(key_of[8], (BR, NA, CF), 1.0, 6.0, ((1, 32),)),
    }


def wrap_columns(values):
    return jnp.concatenate([values[:, -1:], values, values[:, :1]], axis=1)


def pad_rows(values):
    return jnp.pad(values, ((1, 1), (0, 0), (0, 0)))


def conv_taps(padded, weights, row_count, col_count):
    result = None
    for tap_index in range(9):
        down_step = tap_index // 3
        right_step = tap_index % 3
        window = padded[down_step:down_step + row_count, right_step:right_step + col_count]
        partial_value = jnp.dot(window.reshape(row_count * col_count, -1), weights[tap_index], preferred_element_type=jnp.float32)
        result = partial_value if result is None else result + partial_value
    return result.reshape(row_count, col_count, -1)


def conv_back(padded, weights, row_count, col_count):
    result = None
    for tap_index in range(9):
        down_step = tap_index // 3
        right_step = tap_index % 3
        window = padded[2 - down_step:2 - down_step + row_count, 2 - right_step:2 - right_step + col_count]
        partial_value = lax.dot_general(window.reshape(row_count * col_count, -1), weights[tap_index], (((1,), (1,)), ((), ())), preferred_element_type=jnp.float32)
        result = partial_value if result is None else result + partial_value
    return result.reshape(row_count, col_count, -1)


def depth_part(block, depth_weight):
    logits = jnp.einsum("hjc,ck->hjk", block.astype(jnp.float32), depth_weight.astype(jnp.float32))
    softened = jax.nn.softplus(logits) + 0.05
    totals = jnp.sum(softened, axis=2, keepdims=True)
    depth_probs = softened / totals
    probs_low = depth_probs.astype(jnp.bfloat16)
    return logits, totals, depth_probs, probs_low


def reference(image_feats, cam_weights, depth_weight, ray_bins, pillar_sums, pillar_counts, lidar_weight, merge_weight, out_cotangent):
    features = image_feats
    for layer_idx in range(LAYERS):
        conv_out = conv_taps(pad_rows(wrap_columns(features)), cam_weights[layer_idx], ROWS, NCOL)
        features = jax.nn.relu(conv_out).astype(jnp.bfloat16)

    def lift_block(grid, sector):
        begin_col = (sector * COLS_DEV).astype(jnp.int32)
        block = lax.dynamic_slice_in_dim(features, begin_col, COLS_DEV, 1)
        bins = lax.dynamic_slice_in_dim(ray_bins, begin_col, COLS_DEV, 0).reshape(-1)
        logits, totals, depth_probs, probs_low = depth_part(block, depth_weight)
        lifted = jnp.einsum("hjk,hjc->jkc", probs_low.astype(jnp.float32), block.astype(jnp.float32))
        grid = grid + jax.ops.segment_sum(lifted.reshape(-1, C), bins, num_segments=NSECT * BCELL)
        return grid, None

    grid, _ = lax.scan(lift_block, jnp.zeros((NSECT * BCELL, C), jnp.float32), jnp.arange(NSECT, dtype=jnp.int32))
    cam_bev = grid.reshape(NSECT, BR, BA, C).transpose(1, 0, 2, 3).reshape(BR, NA, C).astype(jnp.bfloat16)

    occupied = (pillar_counts > 0).astype(jnp.float32)
    divisor = jnp.maximum(pillar_counts, 1).astype(jnp.float32)
    pillar_feat = (pillar_sums.astype(jnp.float32) * (occupied / divisor)[:, :, None]).astype(jnp.bfloat16)
    grouped = pillar_feat.reshape(BR, 2, NA, 2, CL)
    lidar_sum = None
    for offset in range(4):
        window = grouped[:, offset // 2, :, offset % 2, :].reshape(BR * NA, CL)
        partial_value = jnp.dot(window, lidar_weight[offset], preferred_element_type=jnp.float32)
        lidar_sum = partial_value if lidar_sum is None else lidar_sum + partial_value
    lid_bev = jax.nn.relu(lidar_sum).reshape(BR, NA, CL).astype(jnp.bfloat16)

    merged_in = jnp.concatenate([cam_bev, lid_bev], axis=2)
    pre_act = conv_taps(pad_rows(wrap_columns(merged_in)), merge_weight, BR, NA)
    merged = jax.nn.silu(pre_act).astype(jnp.bfloat16)
    gating = jax.nn.sigmoid(pre_act)
    slopes = gating * (1.0 + pre_act * (1.0 - gating))
    grad_pre = (out_cotangent.astype(jnp.float32) * slopes).astype(jnp.bfloat16)
    grad_in = conv_back(pad_rows(wrap_columns(grad_pre)), merge_weight, BR, NA)
    lid_grad = grad_in[:, :, C:].astype(jnp.bfloat16)
    cam_bev_grad = grad_in[:, :, :C].astype(jnp.bfloat16)
    grad_table = cam_bev_grad.reshape(BR, NSECT, BA, C).transpose(1, 0, 2, 3).reshape(NSECT * BCELL, C)

    def back_block(sector):
        begin_col = (sector * COLS_DEV).astype(jnp.int32)
        block = lax.dynamic_slice_in_dim(features, begin_col, COLS_DEV, 1)
        bins = lax.dynamic_slice_in_dim(ray_bins, begin_col, COLS_DEV, 0).reshape(-1)
        logits, totals, depth_probs, probs_low = depth_part(block, depth_weight)
        grad_lift = jnp.take(grad_table, bins, axis=0).reshape(COLS_DEV, DB, C)
        grad_probs = jnp.einsum("jkc,hjc->hjk", grad_lift.astype(jnp.float32), block.astype(jnp.float32))
        grad_direct = jnp.einsum("hjk,jkc->hjc", probs_low.astype(jnp.float32), grad_lift.astype(jnp.float32))
        grad_soft = (grad_probs - jnp.sum(grad_probs * depth_probs, axis=2, keepdims=True)) / totals
        grad_logits = (grad_soft * jax.nn.sigmoid(logits)).astype(jnp.bfloat16)
        grad_depth = jnp.einsum("hjk,ck->hjc", grad_logits.astype(jnp.float32), depth_weight.astype(jnp.float32))
        return (grad_direct + grad_depth).astype(jnp.bfloat16)

    blocks = lax.map(back_block, jnp.arange(NSECT, dtype=jnp.int32))
    cam_grad = blocks.transpose(1, 0, 2, 3).reshape(ROWS, NCOL, C)
    return merged, cam_grad, lid_grad
```

```python
import functools

import jax
import jax.numpy as jnp
from jax import lax
from jax.experimental import pallas as pl
from jax.experimental.pallas import tpu as pltpu
from jax.sharding import PartitionSpec as P

AXES = ("branch", "strip")
CH = 8


def rolled_sum(low, mid, high, period):
    rows = mid.shape[0]
    place = lax.broadcasted_iota(jnp.int32, mid.shape, 0) & (period - 1)
    down = jnp.where(place == 0, 0.0, pltpu.roll(low, 1, 0))
    up = jnp.where(place == period - 1, 0.0, pltpu.roll(high, rows - 1, 0))
    return mid + down + up


def conv_rows(src, starts, rows, weights, layer, height):
    taps = [
        jnp.concatenate([src[pl.ds(s + i * height, rows), :] for s in starts], axis=0)
        for i in range(3)
    ]
    x = jnp.concatenate(taps, axis=1)
    channels = taps[0].shape[1]
    z = [
        jnp.dot(
            x,
            weights[layer, 3 * dy : 3 * dy + 3].reshape(3 * channels, -1),
            preferred_element_type=jnp.float32,
        )
        for dy in range(3)
    ]
    total = rolled_sum(z[0], z[1], z[2], height)
    return jnp.maximum(total, 0.0).astype(jnp.bfloat16)


def kernel(
    n, strips, cols, height, br, ba, bins_n,
    img, cw, wd, bins, lid, cot, mw,
    merged_o, camgrad_o, lidgrad_o,
    xin, y1, y2, feats, codes, wdp, probs, slope, picker, amat, parts, sendbuf,
    rp1, rp2, rp3, rm1, rm2, rm3, win, lidwin, cotwin, table,
    local_sem, send_sem, recv_sem,
):
    me = lax.axis_index(AXES[0]) * strips + lax.axis_index(AXES[1])
    ch_rows = CH * height
    lanes = wdp.shape[1]

    def dev(d):
        t = lax.rem(me + d + n, n)
        return (t // strips, t % strips)

    barrier = pltpu.get_barrier_semaphore()
    for d in (1, 2, 3, -1, -2, -3):
        pl.semaphore_signal(
            barrier, inc=1, device_id=dev(d), device_id_type=pl.DeviceIdType.MESH
        )
    own = pltpu.make_async_copy(img, xin.at[pl.ds(3 * height, cols * height)], local_sem.at[0])
    own.start()
    own_cot = pltpu.make_async_copy(
        cot, cotwin.at[pl.ds((ba + 1) * br, ba * br)], local_sem.at[1]
    )
    own_cot.start()
    own_lid = pltpu.make_async_copy(
        lid, lidwin.at[pl.ds((ba + 2) * br, ba * br)], local_sem.at[2]
    )
    own_lid.start()

    cell = br * ba
    sh_cell, sh_ba, sh_br = cell.bit_length() - 1, ba.bit_length() - 1, br.bit_length() - 1
    raw = bins[...]
    off = (raw >> sh_cell) - me + 1
    off = jnp.where(off < 0, off + n, off)
    off = jnp.where(off >= n, off - n, off)
    in_cell = raw & (cell - 1)
    code = (((off << sh_ba) + (in_cell & (ba - 1))) << sh_br) + (in_cell >> sh_ba)
    codes[...] = jnp.full(codes.shape, -1, jnp.int32)
    codes[:, 0:bins_n] = code
    wdp[...] = jnp.zeros_like(wdp)
    wdp[:, 0:bins_n] = wd[...]
    parts[...] = jnp.zeros_like(parts)
    own.wait()

    def interior(src, dst, layer, first, shift):
        def step(i, carry):
            c = jnp.minimum(first + CH * i, cols - first - CH) + shift
            at = pl.multiple_of(c * height, height)
            dst[pl.ds(at, ch_rows), :] = conv_rows(src, [at], ch_rows, cw, layer, height)
            return carry

        lax.fori_loop(0, cols // CH, step, 0)

    interior(xin, y1, 0, 1, 2)
    own_cot.wait()
    own_lid.wait()
    pl.semaphore_wait(barrier, 6)

    messages = []

    def send(src, dst, d):
        m = len(messages)
        copy = pltpu.make_async_remote_copy(
            src_ref=src,
            dst_ref=dst,
            send_sem=send_sem.at[m],
            recv_sem=recv_sem.at[m],
            device_id=dev(d),
            device_id_type=pl.DeviceIdType.MESH,
        )
        copy.start()
        messages.append(copy)

    h3 = 3 * height
    send(xin.at[pl.ds(cols * height, h3)], xin.at[pl.ds(0, h3)], 1)
    send(xin.at[pl.ds(h3, h3)], xin.at[pl.ds((cols + 3) * height, h3)], -1)
    sec = ba * br
    send(cot, cotwin.at[pl.ds(br, sec)], 1)
    send(cot, cotwin.at[pl.ds((2 * ba + 1) * br, sec)], -1)
    send(cot.at[pl.ds(sec - br, br)], cotwin.at[pl.ds(0, br)], 2)
    send(cot.at[pl.ds(0, br)], cotwin.at[pl.ds((3 * ba + 1) * br, br)], -2)
    send(lid, lidwin.at[pl.ds(2 * br, sec)], 1)
    send(lid, lidwin.at[pl.ds((2 * ba + 2) * br, sec)], -1)
    send(lid.at[pl.ds(sec - 2 * br, 2 * br)], lidwin.at[pl.ds(0, 2 * br)], 2)
    send(lid.at[pl.ds(0, 2 * br)], lidwin.at[pl.ds((3 * ba + 2) * br, 2 * br)], -2)

    interior(y1, y2, 1, 2, 1)
    interior(y2, feats, 2, 3, 0)

    messages[0].wait_recv()
    messages[1].wait_recv()
    for layer, (src, dst, extra) in enumerate(((xin, y1, 4), (y1, y2, 2), (y2, feats, 0))):
        right = (cols + extra - 3) * height
        edge = conv_rows(src, [0, right], h3, cw, layer, height)
        dst[pl.ds(0, h3), :] = edge[:h3]
        dst[pl.ds(right, h3), :] = edge[h3:]

    groups = amat.shape[1]
    used = 3 * ba * br
    lane = lax.broadcasted_iota(jnp.int32, (ch_rows, lanes), 1)
    row_id = lax.broadcasted_iota(jnp.int32, (groups, lanes), 0)

    def lift(i, carry):
        at = pl.multiple_of(i * ch_rows, ch_rows)
        f = feats[pl.ds(at, ch_rows), :]
        logits = jnp.dot(f, wdp[...], preferred_element_type=jnp.float32)
        e = jnp.exp(-jnp.abs(logits))
        soft = jnp.maximum(logits, 0.0) + jnp.log1p(e) + 0.05
        soft = jnp.where(lane < bins_n, soft, 0.0)
        inv = 1.0 / jnp.sum(soft, axis=1, keepdims=True)
        p = soft * inv
        sig = jnp.where(logits >= 0.0, 1.0, e) / (1.0 + e)
        probs[pl.ds(at, ch_rows), :] = p
        slope[pl.ds(at, ch_rows), :] = jnp.where(lane < bins_n, sig * inv, 0.0)
        low = p.astype(jnp.bfloat16)
        rows = []
        for c in range(CH):
            j = i * CH + c
            pick = jnp.where(row_id == codes[pl.ds(j, 1), :], 1.0, 0.0).astype(jnp.bfloat16)
            picker[j] = pick
            rows.append(
                lax.dot_general(
                    low[c * height : (c + 1) * height],
                    pick,
                    (((1,), (1,)), ((), ())),
                    preferred_element_type=jnp.float32,
                )
            )
        a = jnp.concatenate(rows, axis=0).astype(jnp.bfloat16)
        amat[pl.ds(at, ch_rows), :] = a
        parts[...] += lax.dot_general(
            a, f, (((0,), (0,)), ((), ())), preferred_element_type=jnp.float32
        )
        return carry

    lax.fori_loop(0, cols // CH, lift, 0)

    mine = parts[0:used, :]
    sendbuf[...] = mine.astype(jnp.bfloat16)
    n1, n2, n3 = (2 * ba + 2) * br, (ba + 2) * br, 2 * br
    send(sendbuf.at[pl.ds(used - n1, n1)], rp1, 1)
    send(sendbuf.at[pl.ds(0, n1)], rm1, -1)
    send(sendbuf.at[pl.ds(used - n2, n2)], rp2, 2)
    send(sendbuf.at[pl.ds(0, n2)], rm2, -2)
    send(sendbuf.at[pl.ds(used - n3, n3)], rp3, 3)
    send(sendbuf.at[pl.ds(0, n3)], rm3, -3)
    total = win.shape[0]
    win[...] = jnp.zeros_like(win)
    win[pl.ds(2 * br, used), :] = mine
    for copy in messages[2:]:
        copy.wait_recv()
    for got, size in ((rp1, n1), (rp2, n2), (rp3, n3)):
        win[pl.ds(0, size), :] += got[...].astype(jnp.float32)
    for got, size in ((rm1, n1), (rm2, n2), (rm3, n3)):
        win[pl.ds(total - size, size), :] += got[...].astype(jnp.float32)

    cam = win[...].astype(jnp.bfloat16)
    channels = cam.shape[1]
    joined = jnp.concatenate([cam, lidwin[...]], axis=1)
    cc = joined.shape[1]
    act_rows = total - 2 * br
    x = jnp.concatenate([joined[i * br : i * br + act_rows] for i in range(3)], axis=1)
    z = [
        jnp.dot(
            x,
            mw[3 * dy : 3 * dy + 3].reshape(3 * cc, -1),
            preferred_element_type=jnp.float32,
        )
        for dy in range(3)
    ]
    act = rolled_sum(z[0], z[1], z[2], br)
    gate = 1.0 / (1.0 + jnp.exp(-act))
    begin = (ba + 1) * br
    merged_o[...] = (act * gate)[begin : begin + sec].astype(jnp.bfloat16)
    grad_pre = (
        cotwin[...].astype(jnp.float32) * (gate * (1.0 + act * (1.0 - gate)))
    ).astype(jnp.bfloat16)
    y = []
    for dy in range(3):
        acc = None
        for i in range(3):
            term = lax.dot_general(
                grad_pre[(2 - i) * br : (2 - i) * br + used],
                mw[3 * dy + i],
                (((1,), (1,)), ((), ())),
                preferred_element_type=jnp.float32,
            )
            acc = term if acc is None else acc + term
        y.append(acc)
    grad_in = rolled_sum(y[2], y[1], y[0], br)
    table[...] = jnp.zeros_like(table)
    table[0:used, :] = grad_in[:, :channels].astype(jnp.bfloat16)
    lidgrad_o[...] = grad_in[sec : 2 * sec, channels:].astype(jnp.bfloat16)

    def back(i, carry):
        at = pl.multiple_of(i * ch_rows, ch_rows)
        f = feats[pl.ds(at, ch_rows), :]
        tab = table[...]
        g = lax.dot_general(
            f, tab, (((1,), (1,)), ((), ())), preferred_element_type=jnp.float32
        ).astype(jnp.bfloat16)
        direct = jnp.dot(amat[pl.ds(at, ch_rows), :], tab, preferred_element_type=jnp.float32)
        gp = jnp.concatenate(
            [
                jnp.dot(
                    g[c * height : (c + 1) * height],
                    picker[i * CH + c],
                    preferred_element_type=jnp.float32,
                )
                for c in range(CH)
            ],
            axis=0,
        )
        mean = jnp.sum(gp * probs[pl.ds(at, ch_rows), :], axis=1, keepdims=True)
        gl = ((gp - mean) * slope[pl.ds(at, ch_rows), :]).astype(jnp.bfloat16)
        depth = lax.dot_general(
            gl, wdp[...], (((1,), (1,)), ((), ())), preferred_element_type=jnp.float32
        )
        camgrad_o[pl.ds(at, ch_rows), :] = (direct + depth).astype(jnp.bfloat16)
        return carry

    lax.fori_loop(0, cols // CH, back, 0)
    for copy in messages:
        copy.wait_send()


def local(
    n, strips,
    image_feats, cam_weights, depth_weight, ray_bins, pillar_sums, pillar_counts,
    lidar_weight, merge_weight, out_cotangent,
):
    height, cols, channels = image_feats.shape
    br, ba, cf = out_cotangent.shape
    bins_n = depth_weight.shape[1]
    cl = pillar_sums.shape[2]
    lanes = -(-bins_n // 128) * 128
    groups = -(-3 * ba * br // 128) * 128
    used = 3 * ba * br
    total = (3 * ba + 4) * br
    sec = ba * br
    bf, f32 = jnp.bfloat16, jnp.float32

    img = image_feats.transpose(1, 0, 2).reshape(cols * height, channels)
    cot = out_cotangent.transpose(1, 0, 2).reshape(sec, cf)
    occupied = (pillar_counts > 0).astype(f32)
    divisor = jnp.maximum(pillar_counts, 1).astype(f32)
    pillar_feat = (pillar_sums.astype(f32) * (occupied / divisor)[:, :, None]).astype(bf)
    taps = pillar_feat.reshape(br, 2, ba, 2, cl).transpose(2, 0, 1, 3, 4).reshape(sec, 4 * cl)
    lid = jnp.dot(taps, lidar_weight.reshape(4 * cl, cl), preferred_element_type=f32)
    lid = jax.nn.relu(lid).astype(bf)

    vm = pl.BlockSpec(memory_space=pltpu.VMEM)
    n1, n2, n3 = (2 * ba + 2) * br, (ba + 2) * br, 2 * br
    merged, cam_grad, lid_grad = pl.pallas_call(
        functools.partial(kernel, n, strips, cols, height, br, ba, bins_n),
        out_shape=(
            jax.ShapeDtypeStruct((sec, cf), bf),
            jax.ShapeDtypeStruct((cols * height, channels), bf),
            jax.ShapeDtypeStruct((sec, cl), bf),
        ),
        in_specs=[vm] * 7,
        out_specs=(vm, vm, vm),
        scratch_shapes=[
            pltpu.VMEM(((cols + 6) * height, channels), bf),
            pltpu.VMEM(((cols + 4) * height, channels), bf),
            pltpu.VMEM(((cols + 2) * height, channels), bf),
            pltpu.VMEM((cols * height, channels), bf),
            pltpu.VMEM((cols, lanes), jnp.int32),
            pltpu.VMEM((channels, lanes), bf),
            pltpu.VMEM((cols * height, lanes), f32),
            pltpu.VMEM((cols * height, lanes), f32),
            pltpu.VMEM((cols, groups, lanes), bf),
            pltpu.VMEM((cols * height, groups), bf),
            pltpu.VMEM((groups, channels), f32),
            pltpu.VMEM((used, channels), bf),
            pltpu.VMEM((n1, channels), bf),
            pltpu.VMEM((n2, channels), bf),
            pltpu.VMEM((n3, channels), bf),
            pltpu.VMEM((n1, channels), bf),
            pltpu.VMEM((n2, channels), bf),
            pltpu.VMEM((n3, channels), bf),
            pltpu.VMEM((total, channels), f32),
            pltpu.VMEM((total, cl), bf),
            pltpu.VMEM((total - 2 * br, cf), bf),
            pltpu.VMEM((groups, channels), bf),
            pltpu.SemaphoreType.DMA((3,)),
            pltpu.SemaphoreType.DMA((16,)),
            pltpu.SemaphoreType.DMA((16,)),
        ],
        compiler_params=pltpu.CompilerParams(
            collective_id=0, has_side_effects=True, vmem_limit_bytes=58 * 1024 * 1024
        ),
        name="bev",
    )(img, cam_weights, depth_weight, ray_bins, lid, cot, merge_weight)
    return (
        merged.reshape(ba, br, cf).transpose(1, 0, 2),
        cam_grad.reshape(cols, height, channels).transpose(1, 0, 2),
        lid_grad.reshape(ba, br, cl).transpose(1, 0, 2),
    )


def solution(mesh):
    strips = mesh.shape["strip"]
    n = mesh.shape["branch"] * strips
    placed = (
        P(None, AXES, None),
        P(),
        P(),
        P(AXES, None),
        P(None, AXES, None),
        P(None, AXES),
        P(),
        P(),
        P(None, AXES, None),
    )
    return jax.shard_map(
        functools.partial(local, n, strips),
        mesh=mesh,
        in_specs=placed,
        out_specs=(P(None, AXES, None),) * 3,
        check_vma=False,
    )
```

```python
import functools

import jax
import jax.numpy as jnp
from jax import lax
from jax.experimental import pallas as pl
from jax.experimental.pallas import tpu as pltpu
from jax.sharding import PartitionSpec as P

AXES = ("branch", "strip")
CH = 8


def rolled_sum(low, mid, high, period):
    rows = mid.shape[0]
    place = lax.broadcasted_iota(jnp.int32, mid.shape, 0) & (period - 1)
    down = jnp.where(place == 0, 0.0, pltpu.roll(low, 1, 0))
    up = jnp.where(place == period - 1, 0.0, pltpu.roll(high, rows - 1, 0))
    return mid + down + up


def conv_rows(src, starts, rows, weights, layer, height):
    taps = [
        jnp.concatenate([src[pl.ds(s + i * height, rows), :] for s in starts], axis=0)
        for i in range(3)
    ]
    x = jnp.concatenate(taps, axis=1)
    channels = taps[0].shape[1]
    z = [
        jnp.dot(
            x,
            weights[layer, 3 * dy : 3 * dy + 3].reshape(3 * channels, -1),
            preferred_element_type=jnp.float32,
        )
        for dy in range(3)
    ]
    total = rolled_sum(z[0], z[1], z[2], height)
    return jnp.maximum(total, 0.0).astype(jnp.bfloat16)


def one_hot_rows(rows, sources, source_of):
    p = lax.broadcasted_iota(jnp.int32, (rows, sources), 0)
    q = lax.broadcasted_iota(jnp.int32, (rows, sources), 1)
    return jnp.where(source_of(p) == q, 1.0, 0.0).astype(jnp.bfloat16)


def kernel(
    n, strips, cols, height, br, ba, bins_n,
    img, cw_hbm, wd, bins, pillars, counts, lw, cot, mw_hbm,
    merged_o, camgrad_o, lidgrad_o,
    cw, mw, xin, y1, y2, feats, codes, wdp, probs, slope, picker, amat, parts, sendbuf,
    rp1, rp2, rp3, rm1, rm2, rm3, win, lidwin, cotwin, table,
    local_sem, send_sem, recv_sem,
):
    me = lax.axis_index(AXES[0]) * strips + lax.axis_index(AXES[1])
    ch_rows = CH * height
    lanes = wdp.shape[0]

    def dev(d):
        t = lax.rem(me + d + n, n)
        return (t // strips, t % strips)

    barrier = pltpu.get_barrier_semaphore()
    for d in (1, 2, 3, -1, -2, -3):
        pl.semaphore_signal(
            barrier, inc=1, device_id=dev(d), device_id_type=pl.DeviceIdType.MESH
        )
    layers = cw.shape[0]
    fetches = [
        pltpu.make_async_copy(cw_hbm.at[k], cw.at[k], local_sem.at[k]) for k in range(layers)
    ]
    fetches.append(pltpu.make_async_copy(mw_hbm, mw, local_sem.at[layers]))
    for copy in fetches:
        copy.start()

    sh_h, sh_ch = height.bit_length() - 1, CH.bit_length() - 1
    to_cols = one_hot_rows(
        ch_rows, ch_rows, lambda p: ((p & (height - 1)) << sh_ch) + (p >> sh_h)
    )
    for i in range(cols // CH):
        block = img[:, i * CH : (i + 1) * CH, :].astype(jnp.float32)
        block = block.reshape(ch_rows, -1).astype(jnp.bfloat16)
        turned = jnp.dot(to_cols, block, preferred_element_type=jnp.float32)
        xin[pl.ds((3 + i * CH) * height, ch_rows), :] = turned.astype(jnp.bfloat16)

    sec = ba * br
    cot_own, lid_own = (ba + 1) * br, (ba + 2) * br
    cot_f = cot[...].astype(jnp.float32)
    for a in range(ba):
        cotwin[pl.ds(cot_own + a * br, br), :] = cot_f[:, a, :].astype(jnp.bfloat16)
    points = counts[...]
    scale = (points > 0).astype(jnp.float32) / jnp.maximum(points, 1).astype(jnp.float32)
    pil = pillars[...].astype(jnp.float32)
    pil = jnp.concatenate(
        [pil[k] * scale[:, k : k + 1] for k in range(2 * br)], axis=0
    ).astype(jnp.bfloat16)
    lb, la = br.bit_length() - 1, ba.bit_length() - 1

    def pillar_row(p):
        r, a, uv = p & (br - 1), (p >> lb) & (ba - 1), p >> (lb + la)
        return ((2 * r + (uv >> 1)) << (la + 1)) + 2 * a + (uv & 1)

    gathered = jnp.dot(
        one_hot_rows(4 * sec, 4 * sec, pillar_row), pil, preferred_element_type=jnp.float32
    ).astype(jnp.bfloat16)
    taps = jnp.concatenate([gathered[k * sec : (k + 1) * sec] for k in range(4)], axis=1)
    lid = jnp.dot(
        taps, lw[...].reshape(taps.shape[1], -1), preferred_element_type=jnp.float32
    )
    lidwin[pl.ds(lid_own, sec), :] = jnp.maximum(lid, 0.0).astype(jnp.bfloat16)

    cell = br * ba
    sh_cell, sh_ba, sh_br = cell.bit_length() - 1, ba.bit_length() - 1, br.bit_length() - 1
    raw = bins[...]
    off = (raw >> sh_cell) - me + 1
    off = jnp.where(off < 0, off + n, off)
    off = jnp.where(off >= n, off - n, off)
    in_cell = raw & (cell - 1)
    code = (((off << sh_ba) + (in_cell & (ba - 1))) << sh_br) + (in_cell >> sh_ba)
    codes[...] = jnp.full(codes.shape, -1, jnp.int32)
    codes[:, 0:bins_n] = code
    wdp[...] = jnp.zeros_like(wdp)
    wdp[0:bins_n, :] = wd[...]
    parts[...] = jnp.zeros_like(parts)
    fetches[0].wait()

    def interior(src, dst, layer, first, shift):
        def step(i, carry):
            c = jnp.minimum(first + CH * i, cols - first - CH) + shift
            at = pl.multiple_of(c * height, height)
            dst[pl.ds(at, ch_rows), :] = conv_rows(src, [at], ch_rows, cw, layer, height)
            return carry

        lax.fori_loop(0, cols // CH, step, 0)

    interior(xin, y1, 0, 1, 2)
    pl.semaphore_wait(barrier, 6)

    messages = []

    def send(src, dst, d):
        m = len(messages)
        copy = pltpu.make_async_remote_copy(
            src_ref=src,
            dst_ref=dst,
            send_sem=send_sem.at[m],
            recv_sem=recv_sem.at[m],
            device_id=dev(d),
            device_id_type=pl.DeviceIdType.MESH,
        )
        copy.start()
        messages.append(copy)

    h3 = 3 * height
    send(xin.at[pl.ds(cols * height, h3)], xin.at[pl.ds(0, h3)], 1)
    send(xin.at[pl.ds(h3, h3)], xin.at[pl.ds((cols + 3) * height, h3)], -1)
    for window, start, edge in ((cotwin, cot_own, br), (lidwin, lid_own, 2 * br)):
        mine = window.at[pl.ds(start, sec)]
        send(mine, window.at[pl.ds(edge, sec)], 1)
        send(mine, window.at[pl.ds(start + sec, sec)], -1)
        last = window.at[pl.ds(start + sec - edge, edge)]
        send(last, window.at[pl.ds(0, edge)], 2)
        send(window.at[pl.ds(start, edge)], window.at[pl.ds(start + 2 * sec, edge)], -2)

    fetches[1].wait()
    interior(y1, y2, 1, 2, 1)
    fetches[2].wait()
    interior(y2, feats, 2, 3, 0)

    messages[0].wait_recv()
    messages[1].wait_recv()
    for layer, (src, dst, extra) in enumerate(((xin, y1, 4), (y1, y2, 2), (y2, feats, 0))):
        right = (cols + extra - 3) * height
        edge = conv_rows(src, [0, right], h3, cw, layer, height)
        dst[pl.ds(0, h3), :] = edge[:h3]
        dst[pl.ds(right, h3), :] = edge[h3:]

    groups = amat.shape[1]
    used = 3 * ba * br
    lane = lax.broadcasted_iota(jnp.int32, (ch_rows, lanes), 1)
    row_id = lax.broadcasted_iota(jnp.int32, (groups, lanes), 0)

    def lift(i, carry):
        at = pl.multiple_of(i * ch_rows, ch_rows)
        f = feats[pl.ds(at, ch_rows), :]
        logits = lax.dot_general(
            f, wdp[...], (((1,), (1,)), ((), ())), preferred_element_type=jnp.float32
        )
        e = jnp.exp(-jnp.abs(logits))
        soft = jnp.maximum(logits, 0.0) + jnp.log1p(e) + 0.05
        soft = jnp.where(lane < bins_n, soft, 0.0)
        inv = 1.0 / jnp.sum(soft, axis=1, keepdims=True)
        p = soft * inv
        sig = jnp.where(logits >= 0.0, 1.0, e) / (1.0 + e)
        probs[pl.ds(at, ch_rows), :] = p
        slope[pl.ds(at, ch_rows), :] = jnp.where(lane < bins_n, sig * inv, 0.0)
        low = p.astype(jnp.bfloat16)
        rows = []
        for c in range(CH):
            j = i * CH + c
            pick = jnp.where(row_id == codes[pl.ds(j, 1), :], 1.0, 0.0).astype(jnp.bfloat16)
            picker[j] = pick
            rows.append(
                lax.dot_general(
                    low[c * height : (c + 1) * height],
                    pick,
                    (((1,), (1,)), ((), ())),
                    preferred_element_type=jnp.float32,
                )
            )
        a = jnp.concatenate(rows, axis=0).astype(jnp.bfloat16)
        amat[pl.ds(at, ch_rows), :] = a
        parts[...] += lax.dot_general(
            a, f, (((0,), (0,)), ((), ())), preferred_element_type=jnp.float32
        )
        return carry

    lax.fori_loop(0, cols // CH, lift, 0)

    mine = parts[0:used, :]
    sendbuf[...] = mine.astype(jnp.bfloat16)
    n1, n2, n3 = (2 * ba + 2) * br, (ba + 2) * br, 2 * br
    send(sendbuf.at[pl.ds(used - n1, n1)], rp1, 1)
    send(sendbuf.at[pl.ds(0, n1)], rm1, -1)
    send(sendbuf.at[pl.ds(used - n2, n2)], rp2, 2)
    send(sendbuf.at[pl.ds(0, n2)], rm2, -2)
    send(sendbuf.at[pl.ds(used - n3, n3)], rp3, 3)
    send(sendbuf.at[pl.ds(0, n3)], rm3, -3)
    total = win.shape[0]
    win[...] = jnp.zeros_like(win)
    win[pl.ds(2 * br, used), :] = mine
    fetches[layers].wait()
    for copy in messages[2:]:
        copy.wait_recv()
    for got, size in ((rp1, n1), (rp2, n2), (rp3, n3)):
        win[pl.ds(0, size), :] += got[...].astype(jnp.float32)
    for got, size in ((rm1, n1), (rm2, n2), (rm3, n3)):
        win[pl.ds(total - size, size), :] += got[...].astype(jnp.float32)

    cam = win[...].astype(jnp.bfloat16)
    channels = cam.shape[1]
    joined = jnp.concatenate([cam, lidwin[...]], axis=1)
    cc = joined.shape[1]
    act_rows = total - 2 * br
    x = jnp.concatenate([joined[i * br : i * br + act_rows] for i in range(3)], axis=1)
    z = [
        jnp.dot(
            x,
            mw[3 * dy : 3 * dy + 3].reshape(3 * cc, -1),
            preferred_element_type=jnp.float32,
        )
        for dy in range(3)
    ]
    act = rolled_sum(z[0], z[1], z[2], br)
    gate = 1.0 / (1.0 + jnp.exp(-act))
    merged = (act * gate)[cot_own : cot_own + sec]
    merged_o[...] = jnp.stack(
        [merged[a * br : (a + 1) * br] for a in range(ba)], axis=1
    ).astype(jnp.bfloat16)
    grad_pre = (
        cotwin[...].astype(jnp.float32) * (gate * (1.0 + act * (1.0 - gate)))
    ).astype(jnp.bfloat16)
    y = []
    for dy in range(3):
        acc = None
        for i in range(3):
            term = lax.dot_general(
                grad_pre[(2 - i) * br : (2 - i) * br + used],
                mw[3 * dy + i],
                (((1,), (1,)), ((), ())),
                preferred_element_type=jnp.float32,
            )
            acc = term if acc is None else acc + term
        y.append(acc)
    grad_in = rolled_sum(y[2], y[1], y[0], br)
    table[...] = jnp.zeros_like(table)
    table[0:used, :] = grad_in[:, :channels].astype(jnp.bfloat16)
    lid_grad = grad_in[sec : 2 * sec, channels:]
    lidgrad_o[...] = jnp.stack(
        [lid_grad[a * br : (a + 1) * br] for a in range(ba)], axis=1
    ).astype(jnp.bfloat16)
    to_rows = one_hot_rows(
        ch_rows, ch_rows, lambda p: ((p & (CH - 1)) << sh_h) + (p >> sh_ch)
    )

    def back(i, carry):
        at = pl.multiple_of(i * ch_rows, ch_rows)
        f = feats[pl.ds(at, ch_rows), :]
        tab = table[...]
        g = lax.dot_general(
            f, tab, (((1,), (1,)), ((), ())), preferred_element_type=jnp.float32
        ).astype(jnp.bfloat16)
        direct = jnp.dot(amat[pl.ds(at, ch_rows), :], tab, preferred_element_type=jnp.float32)
        gp = jnp.concatenate(
            [
                jnp.dot(
                    g[c * height : (c + 1) * height],
                    picker[i * CH + c],
                    preferred_element_type=jnp.float32,
                )
                for c in range(CH)
            ],
            axis=0,
        )
        mean = jnp.sum(gp * probs[pl.ds(at, ch_rows), :], axis=1, keepdims=True)
        gl = ((gp - mean) * slope[pl.ds(at, ch_rows), :]).astype(jnp.bfloat16)
        depth = jnp.dot(gl, wdp[...], preferred_element_type=jnp.float32)
        block = (direct + depth).astype(jnp.bfloat16)
        turned = jnp.dot(to_rows, block, preferred_element_type=jnp.float32)
        camgrad_o[:, pl.ds(pl.multiple_of(i * CH, CH), CH), :] = turned.reshape(
            height, CH, -1
        ).astype(jnp.bfloat16)
        return carry

    lax.fori_loop(0, cols // CH, back, 0)
    for copy in messages:
        copy.wait_send()


def local(
    n, strips,
    image_feats, cam_weights, depth_weight, ray_bins, pillar_sums, pillar_counts,
    lidar_weight, merge_weight, out_cotangent,
):
    height, cols, channels = image_feats.shape
    br, ba, cf = out_cotangent.shape
    bins_n = depth_weight.shape[1]
    cl = pillar_sums.shape[2]
    lanes = -(-bins_n // 128) * 128
    groups = -(-3 * ba * br // 128) * 128
    used = 3 * ba * br
    total = (3 * ba + 4) * br
    bf, f32 = jnp.bfloat16, jnp.float32

    vm = pl.BlockSpec(memory_space=pltpu.VMEM)
    hbm = pl.BlockSpec(memory_space=pl.ANY)
    n1, n2, n3 = (2 * ba + 2) * br, (ba + 2) * br, 2 * br
    return pl.pallas_call(
        functools.partial(kernel, n, strips, cols, height, br, ba, bins_n),
        out_shape=(
            jax.ShapeDtypeStruct((br, ba, cf), bf),
            jax.ShapeDtypeStruct((height, cols, channels), bf),
            jax.ShapeDtypeStruct((br, ba, cl), bf),
        ),
        in_specs=[vm, hbm, vm, vm, vm, vm, vm, vm, hbm],
        out_specs=(vm, vm, vm),
        scratch_shapes=[
            pltpu.VMEM(cam_weights.shape, bf),
            pltpu.VMEM(merge_weight.shape, bf),
            pltpu.VMEM(((cols + 6) * height, channels), bf),
            pltpu.VMEM(((cols + 4) * height, channels), bf),
            pltpu.VMEM(((cols + 2) * height, channels), bf),
            pltpu.VMEM((cols * height, channels), bf),
            pltpu.VMEM((cols, lanes), jnp.int32),
            pltpu.VMEM((lanes, channels), bf),
            pltpu.VMEM((cols * height, lanes), f32),
            pltpu.VMEM((cols * height, lanes), f32),
            pltpu.VMEM((cols, groups, lanes), bf),
            pltpu.VMEM((cols * height, groups), bf),
            pltpu.VMEM((groups, channels), f32),
            pltpu.VMEM((used, channels), bf),
            pltpu.VMEM((n1, channels), bf),
            pltpu.VMEM((n2, channels), bf),
            pltpu.VMEM((n3, channels), bf),
            pltpu.VMEM((n1, channels), bf),
            pltpu.VMEM((n2, channels), bf),
            pltpu.VMEM((n3, channels), bf),
            pltpu.VMEM((total, channels), f32),
            pltpu.VMEM((total, cl), bf),
            pltpu.VMEM((total - 2 * br, cf), bf),
            pltpu.VMEM((groups, channels), bf),
            pltpu.SemaphoreType.DMA((cam_weights.shape[0] + 1,)),
            pltpu.SemaphoreType.DMA((16,)),
            pltpu.SemaphoreType.DMA((16,)),
        ],
        compiler_params=pltpu.CompilerParams(
            collective_id=0, has_side_effects=True, vmem_limit_bytes=58 * 1024 * 1024
        ),
        name="bev",
    )(
        image_feats, cam_weights, depth_weight.T, ray_bins, pillar_sums, pillar_counts.T,
        lidar_weight, out_cotangent, merge_weight,
    )


def solution(mesh):
    strips = mesh.shape["strip"]
    n = mesh.shape["branch"] * strips
    placed = (
        P(None, AXES, None),
        P(),
        P(),
        P(AXES, None),
        P(None, AXES, None),
        P(None, AXES),
        P(),
        P(),
        P(None, AXES, None),
    )
    return jax.shard_map(
        functools.partial(local, n, strips),
        mesh=mesh,
        in_specs=placed,
        out_specs=(P(None, AXES, None),) * 3,
        check_vma=False,
    )
```

```python
import functools

import jax
import jax.numpy as jnp
from jax import lax
from jax.experimental import pallas as pl
from jax.experimental.pallas import tpu as pltpu
from jax.sharding import PartitionSpec as P

AXES = ("branch", "strip")
CH = 8


def rolled_sum(low, mid, high, period):
    rows = mid.shape[0]
    place = lax.broadcasted_iota(jnp.int32, mid.shape, 0) & (period - 1)
    down = jnp.where(place == 0, 0.0, pltpu.roll(low, 1, 0))
    up = jnp.where(place == period - 1, 0.0, pltpu.roll(high, rows - 1, 0))
    return mid + down + up


def conv_rows(src, starts, rows, weights, layer, height):
    taps = [
        jnp.concatenate([src[pl.ds(s + i * height, rows), :] for s in starts], axis=0)
        for i in range(3)
    ]
    x = jnp.concatenate(taps, axis=1)
    channels = taps[0].shape[1]
    z = [
        jnp.dot(
            x,
            weights[layer, 3 * dy : 3 * dy + 3].reshape(3 * channels, -1),
            preferred_element_type=jnp.float32,
        )
        for dy in range(3)
    ]
    total = rolled_sum(z[0], z[1], z[2], height)
    return jnp.maximum(total, 0.0).astype(jnp.bfloat16)


def one_hot_rows(rows, sources, source_of):
    p = lax.broadcasted_iota(jnp.int32, (rows, sources), 0)
    q = lax.broadcasted_iota(jnp.int32, (rows, sources), 1)
    return jnp.where(source_of(p) == q, 1.0, 0.0).astype(jnp.bfloat16)


def row_numbers(shape):
    return lax.broadcasted_iota(jnp.int32, shape, 0).astype(jnp.float32).astype(jnp.bfloat16)


def pick_of(row_id, codes, j):
    groups, lanes = row_id.shape
    code = jnp.broadcast_to(codes[pl.ds(j, 1), :], (16, lanes)).astype(jnp.bfloat16)
    code = jnp.concatenate([code] * (groups // 16), axis=0)
    one, zero = jnp.ones((), jnp.bfloat16), jnp.zeros((), jnp.bfloat16)
    return jnp.where(row_id[...] == code, one, zero)


def kernel(
    n, strips, cols, height, br, ba, bins_n,
    img, cw_hbm, wd, bins, pillars, counts, lw, cot, mw_hbm,
    merged_o, lidgrad_o, table, codes, feats_o, amat_o, probs_o, slope_o,
    cw, mw, xin, y1, y2, feats, wdp, probs, slope, low, row_id, amat, parts, sendbuf,
    rp1, rp2, rp3, rm1, rm2, rm3, win, lidwin, cotwin,
    local_sem, out_sem, send_sem, recv_sem,
):
    me = lax.axis_index(AXES[0]) * strips + lax.axis_index(AXES[1])
    ch_rows = CH * height
    lanes = wdp.shape[0]

    def dev(d):
        t = lax.rem(me + d + n, n)
        return (t // strips, t % strips)

    barrier = pltpu.get_barrier_semaphore()
    for d in (1, 2, 3, -1, -2, -3):
        pl.semaphore_signal(
            barrier, inc=1, device_id=dev(d), device_id_type=pl.DeviceIdType.MESH
        )
    layers = cw.shape[0]
    fetches = [
        pltpu.make_async_copy(cw_hbm.at[k], cw.at[k], local_sem.at[k]) for k in range(layers)
    ]
    fetches.append(pltpu.make_async_copy(mw_hbm, mw, local_sem.at[layers]))
    for copy in fetches:
        copy.start()

    sh_h, sh_ch = height.bit_length() - 1, CH.bit_length() - 1
    to_cols = one_hot_rows(
        ch_rows, ch_rows, lambda p: ((p & (height - 1)) << sh_ch) + (p >> sh_h)
    )
    for i in range(cols // CH):
        block = img[:, i * CH : (i + 1) * CH, :].astype(jnp.float32)
        block = block.reshape(ch_rows, -1).astype(jnp.bfloat16)
        turned = jnp.dot(to_cols, block, preferred_element_type=jnp.float32)
        xin[pl.ds((3 + i * CH) * height, ch_rows), :] = turned.astype(jnp.bfloat16)

    sec = ba * br
    cot_own, lid_own = (ba + 1) * br, (ba + 2) * br
    cot_f = cot[...].astype(jnp.float32)
    for a in range(ba):
        cotwin[pl.ds(cot_own + a * br, br), :] = cot_f[:, a, :].astype(jnp.bfloat16)
    points = counts[...]
    scale = (points > 0).astype(jnp.float32) / jnp.maximum(points, 1).astype(jnp.float32)
    pil = pillars[...].astype(jnp.float32)
    pil = jnp.concatenate(
        [pil[k] * scale[:, k : k + 1] for k in range(2 * br)], axis=0
    ).astype(jnp.bfloat16)
    lb, la = br.bit_length() - 1, ba.bit_length() - 1

    def pillar_row(p):
        r, a, uv = p & (br - 1), (p >> lb) & (ba - 1), p >> (lb + la)
        return ((2 * r + (uv >> 1)) << (la + 1)) + 2 * a + (uv & 1)

    gathered = jnp.dot(
        one_hot_rows(4 * sec, 4 * sec, pillar_row), pil, preferred_element_type=jnp.float32
    ).astype(jnp.bfloat16)
    taps = jnp.concatenate([gathered[k * sec : (k + 1) * sec] for k in range(4)], axis=1)
    lid = jnp.dot(
        taps, lw[...].reshape(taps.shape[1], -1), preferred_element_type=jnp.float32
    )
    lidwin[pl.ds(lid_own, sec), :] = jnp.maximum(lid, 0.0).astype(jnp.bfloat16)

    cell = br * ba
    sh_cell, sh_ba, sh_br = cell.bit_length() - 1, ba.bit_length() - 1, br.bit_length() - 1
    raw = bins[...]
    off = (raw >> sh_cell) - me + 1
    off = jnp.where(off < 0, off + n, off)
    off = jnp.where(off >= n, off - n, off)
    in_cell = raw & (cell - 1)
    code = (((off << sh_ba) + (in_cell & (ba - 1))) << sh_br) + (in_cell >> sh_ba)
    codes[...] = jnp.full(codes.shape, -1.0, jnp.float32)
    codes[:, 0:bins_n] = code.astype(jnp.float32)
    row_id[...] = row_numbers(row_id.shape)
    wdp[...] = jnp.zeros_like(wdp)
    wdp[0:bins_n, :] = wd[...]
    parts[...] = jnp.zeros_like(parts)
    fetches[0].wait()

    def interior(src, dst, layer, first, shift):
        def step(i, carry):
            c = jnp.minimum(first + CH * i, cols - first - CH) + shift
            at = pl.multiple_of(c * height, height)
            dst[pl.ds(at, ch_rows), :] = conv_rows(src, [at], ch_rows, cw, layer, height)
            return carry

        lax.fori_loop(0, cols // CH, step, 0)

    interior(xin, y1, 0, 1, 2)
    pl.semaphore_wait(barrier, 6)

    messages = []

    def send(src, dst, d):
        m = len(messages)
        copy = pltpu.make_async_remote_copy(
            src_ref=src,
            dst_ref=dst,
            send_sem=send_sem.at[m],
            recv_sem=recv_sem.at[m],
            device_id=dev(d),
            device_id_type=pl.DeviceIdType.MESH,
        )
        copy.start()
        messages.append(copy)

    h3 = 3 * height
    send(xin.at[pl.ds(cols * height, h3)], xin.at[pl.ds(0, h3)], 1)
    send(xin.at[pl.ds(h3, h3)], xin.at[pl.ds((cols + 3) * height, h3)], -1)
    for window, start, edge in ((cotwin, cot_own, br), (lidwin, lid_own, 2 * br)):
        mine = window.at[pl.ds(start, sec)]
        send(mine, window.at[pl.ds(edge, sec)], 1)
        send(mine, window.at[pl.ds(start + sec, sec)], -1)
        last = window.at[pl.ds(start + sec - edge, edge)]
        send(last, window.at[pl.ds(0, edge)], 2)
        send(window.at[pl.ds(start, edge)], window.at[pl.ds(start + 2 * sec, edge)], -2)

    fetches[1].wait()
    interior(y1, y2, 1, 2, 1)
    fetches[2].wait()
    interior(y2, feats, 2, 3, 0)

    messages[0].wait_recv()
    messages[1].wait_recv()
    for layer, (src, dst, extra) in enumerate(((xin, y1, 4), (y1, y2, 2), (y2, feats, 0))):
        right = (cols + extra - 3) * height
        edge = conv_rows(src, [0, right], h3, cw, layer, height)
        dst[pl.ds(0, h3), :] = edge[:h3]
        dst[pl.ds(right, h3), :] = edge[h3:]

    outs = []

    def write(src, dst):
        copy = pltpu.make_async_copy(src, dst, out_sem.at[len(outs)])
        copy.start()
        outs.append(copy)

    used = 3 * ba * br
    lane = lax.broadcasted_iota(jnp.int32, (ch_rows, lanes), 1)

    def soften(i, carry):
        at = pl.multiple_of(i * ch_rows, ch_rows)
        f = feats[pl.ds(at, ch_rows), :]
        logits = lax.dot_general(
            f, wdp[...], (((1,), (1,)), ((), ())), preferred_element_type=jnp.float32
        )
        e = jnp.exp(-jnp.abs(logits))
        soft = jnp.maximum(logits, 0.0) + jnp.log1p(e) + 0.05
        soft = jnp.where(lane < bins_n, soft, 0.0)
        inv = 1.0 / jnp.sum(soft, axis=1, keepdims=True)
        p = soft * inv
        sig = jnp.where(logits >= 0.0, 1.0, e) / (1.0 + e)
        probs[pl.ds(at, ch_rows), :] = p
        slope[pl.ds(at, ch_rows), :] = jnp.where(lane < bins_n, sig * inv, 0.0)
        low[pl.ds(at, ch_rows), :] = p.astype(jnp.bfloat16)
        return carry

    lax.fori_loop(0, cols // CH, soften, 0)

    def lift(i, carry):
        for c in range(CH):
            j = i * CH + c
            at = pl.multiple_of(j * height, height)
            a = lax.dot_general(
                low[pl.ds(at, height), :],
                pick_of(row_id, codes, j),
                (((1,), (1,)), ((), ())),
                preferred_element_type=jnp.float32,
            )
            amat[pl.ds(at, height), :] = a.astype(jnp.bfloat16)
        return carry

    lax.fori_loop(0, cols // CH, lift, 0)

    def gather(i, carry):
        at = pl.multiple_of(i * 2 * ch_rows, 2 * ch_rows)
        parts[...] += lax.dot_general(
            amat[pl.ds(at, 2 * ch_rows), :],
            feats[pl.ds(at, 2 * ch_rows), :],
            (((0,), (0,)), ((), ())),
            preferred_element_type=jnp.float32,
        )
        return carry

    lax.fori_loop(0, cols // (2 * CH), gather, 0)

    mine = parts[0:used, :]
    sendbuf[...] = mine.astype(jnp.bfloat16)
    n1, n2, n3 = (2 * ba + 2) * br, (ba + 2) * br, 2 * br
    send(sendbuf.at[pl.ds(used - n1, n1)], rp1, 1)
    send(sendbuf.at[pl.ds(0, n1)], rm1, -1)
    send(sendbuf.at[pl.ds(used - n2, n2)], rp2, 2)
    send(sendbuf.at[pl.ds(0, n2)], rm2, -2)
    send(sendbuf.at[pl.ds(used - n3, n3)], rp3, 3)
    send(sendbuf.at[pl.ds(0, n3)], rm3, -3)
    write(feats, feats_o)
    write(amat, amat_o)
    write(probs, probs_o)
    write(slope, slope_o)
    total = win.shape[0]
    win[...] = jnp.zeros_like(win)
    win[pl.ds(2 * br, used), :] = mine
    fetches[layers].wait()
    for copy in messages[2:]:
        copy.wait_recv()
    for got, size in ((rp1, n1), (rp2, n2), (rp3, n3)):
        win[pl.ds(0, size), :] += got[...].astype(jnp.float32)
    for got, size in ((rm1, n1), (rm2, n2), (rm3, n3)):
        win[pl.ds(total - size, size), :] += got[...].astype(jnp.float32)

    cam = win[...].astype(jnp.bfloat16)
    channels = cam.shape[1]
    joined = jnp.concatenate([cam, lidwin[...]], axis=1)
    cc = joined.shape[1]
    act_rows = total - 2 * br
    x = jnp.concatenate([joined[i * br : i * br + act_rows] for i in range(3)], axis=1)
    z = [
        jnp.dot(
            x,
            mw[3 * dy : 3 * dy + 3].reshape(3 * cc, -1),
            preferred_element_type=jnp.float32,
        )
        for dy in range(3)
    ]
    act = rolled_sum(z[0], z[1], z[2], br)
    gate = 1.0 / (1.0 + jnp.exp(-act))
    merged = (act * gate)[cot_own : cot_own + sec]
    merged_o[...] = jnp.stack(
        [merged[a * br : (a + 1) * br] for a in range(ba)], axis=1
    ).astype(jnp.bfloat16)
    grad_pre = (
        cotwin[...].astype(jnp.float32) * (gate * (1.0 + act * (1.0 - gate)))
    ).astype(jnp.bfloat16)
    y = []
    for dy in range(3):
        acc = None
        for i in range(3):
            term = lax.dot_general(
                grad_pre[(2 - i) * br : (2 - i) * br + used],
                mw[3 * dy + i],
                (((1,), (1,)), ((), ())),
                preferred_element_type=jnp.float32,
            )
            acc = term if acc is None else acc + term
        y.append(acc)
    grad_in = rolled_sum(y[2], y[1], y[0], br)
    table[...] = jnp.zeros_like(table)
    table[0:used, :] = grad_in[:, :channels].astype(jnp.bfloat16)
    lid_grad = grad_in[sec : 2 * sec, channels:]
    lidgrad_o[...] = jnp.stack(
        [lid_grad[a * br : (a + 1) * br] for a in range(ba)], axis=1
    ).astype(jnp.bfloat16)
    for copy in messages:
        copy.wait_send()
    for copy in outs:
        copy.wait()


def back_kernel(
    height, bins_n,
    feats, amat, probs, slope, codes, table, wd, merged, lid_grad,
    camgrad_o, merged_o, lidgrad_o,
    wdp, row_id,
):
    step = pl.program_id(0)
    ch_rows = CH * height
    sh_h, sh_ch = height.bit_length() - 1, CH.bit_length() - 1

    @pl.when(step == 0)
    def _():
        merged_o[...] = merged[...]
        lidgrad_o[...] = lid_grad[...]
        wdp[...] = jnp.zeros_like(wdp)
        wdp[0:bins_n, :] = wd[...]
        row_id[...] = row_numbers(row_id.shape)

    to_rows = one_hot_rows(
        ch_rows, ch_rows, lambda p: ((p & (CH - 1)) << sh_h) + (p >> sh_ch)
    )
    chunks = feats.shape[0] // ch_rows
    tab = table[...]
    for k in range(chunks):
        rows = pl.ds(k * ch_rows, ch_rows)
        g = lax.dot_general(
            feats[rows, :], tab, (((1,), (1,)), ((), ())), preferred_element_type=jnp.float32
        ).astype(jnp.bfloat16)
        direct = jnp.dot(amat[rows, :], tab, preferred_element_type=jnp.float32)
        gp = jnp.concatenate(
            [
                jnp.dot(
                    g[c * height : (c + 1) * height],
                    pick_of(row_id, codes, (step * chunks + k) * CH + c),
                    preferred_element_type=jnp.float32,
                )
                for c in range(CH)
            ],
            axis=0,
        )
        mean = jnp.sum(gp * probs[rows, :], axis=1, keepdims=True)
        gl = ((gp - mean) * slope[rows, :]).astype(jnp.bfloat16)
        depth = jnp.dot(gl, wdp[...], preferred_element_type=jnp.float32)
        block = (direct + depth).astype(jnp.bfloat16)
        turned = jnp.dot(to_rows, block, preferred_element_type=jnp.float32)
        camgrad_o[:, k * CH : (k + 1) * CH, :] = turned.reshape(height, CH, -1).astype(
            jnp.bfloat16
        )


def local(
    n, strips,
    image_feats, cam_weights, depth_weight, ray_bins, pillar_sums, pillar_counts,
    lidar_weight, merge_weight, out_cotangent,
):
    height, cols, channels = image_feats.shape
    br, ba, cf = out_cotangent.shape
    bins_n = depth_weight.shape[1]
    cl = pillar_sums.shape[2]
    lanes = -(-bins_n // 128) * 128
    groups = -(-3 * ba * br // 128) * 128
    used = 3 * ba * br
    total = (3 * ba + 4) * br
    bf, f32 = jnp.bfloat16, jnp.float32

    vm = pl.BlockSpec(memory_space=pltpu.VMEM)
    hbm = pl.BlockSpec(memory_space=pl.ANY)
    n1, n2, n3 = (2 * ba + 2) * br, (ba + 2) * br, 2 * br
    rows = cols * height
    merged, lid_grad, table, codes, feats, amat, probs, slope = pl.pallas_call(
        functools.partial(kernel, n, strips, cols, height, br, ba, bins_n),
        out_shape=(
            jax.ShapeDtypeStruct((br, ba, cf), bf),
            jax.ShapeDtypeStruct((br, ba, cl), bf),
            jax.ShapeDtypeStruct((groups, channels), bf),
            jax.ShapeDtypeStruct((cols, lanes), f32),
            jax.ShapeDtypeStruct((rows, channels), bf),
            jax.ShapeDtypeStruct((rows, groups), bf),
            jax.ShapeDtypeStruct((rows, lanes), f32),
            jax.ShapeDtypeStruct((rows, lanes), f32),
        ),
        in_specs=[vm, hbm, vm, vm, vm, vm, vm, vm, hbm],
        out_specs=(vm,) * 4 + (hbm,) * 4,
        scratch_shapes=[
            pltpu.VMEM(cam_weights.shape, bf),
            pltpu.VMEM(merge_weight.shape, bf),
            pltpu.VMEM(((cols + 6) * height, channels), bf),
            pltpu.VMEM(((cols + 4) * height, channels), bf),
            pltpu.VMEM(((cols + 2) * height, channels), bf),
            pltpu.VMEM((cols * height, channels), bf),
            pltpu.VMEM((lanes, channels), bf),
            pltpu.VMEM((cols * height, lanes), f32),
            pltpu.VMEM((cols * height, lanes), f32),
            pltpu.VMEM((cols * height, lanes), bf),
            pltpu.VMEM((groups, lanes), bf),
            pltpu.VMEM((cols * height, groups), bf),
            pltpu.VMEM((groups, channels), f32),
            pltpu.VMEM((used, channels), bf),
            pltpu.VMEM((n1, channels), bf),
            pltpu.VMEM((n2, channels), bf),
            pltpu.VMEM((n3, channels), bf),
            pltpu.VMEM((n1, channels), bf),
            pltpu.VMEM((n2, channels), bf),
            pltpu.VMEM((n3, channels), bf),
            pltpu.VMEM((total, channels), f32),
            pltpu.VMEM((total, cl), bf),
            pltpu.VMEM((total - 2 * br, cf), bf),
            pltpu.SemaphoreType.DMA((cam_weights.shape[0] + 1,)),
            pltpu.SemaphoreType.DMA((4,)),
            pltpu.SemaphoreType.DMA((16,)),
            pltpu.SemaphoreType.DMA((16,)),
        ],
        compiler_params=pltpu.CompilerParams(
            collective_id=0, has_side_effects=True, vmem_limit_bytes=58 * 1024 * 1024
        ),
        name="bev",
    )(
        image_feats, cam_weights, depth_weight.T, ray_bins, pillar_sums, pillar_counts.T,
        lidar_weight, out_cotangent, merge_weight,
    )
    steps = cols // (2 * CH)

    def rowed(width):
        return pl.BlockSpec((rows // steps, width), lambda i: (i, 0))

    def whole(*shape):
        return pl.BlockSpec(shape, lambda i: (0,) * len(shape))

    cam_grad, merged, lid_grad = pl.pallas_call(
        functools.partial(back_kernel, height, bins_n),
        grid=(steps,),
        out_shape=(
            jax.ShapeDtypeStruct((height, cols, channels), bf),
            jax.ShapeDtypeStruct((br, ba, cf), bf),
            jax.ShapeDtypeStruct((br, ba, cl), bf),
        ),
        in_specs=[
            rowed(channels), rowed(groups), rowed(lanes), rowed(lanes),
            whole(cols, lanes), whole(groups, channels), whole(bins_n, channels),
            whole(br, ba, cf), whole(br, ba, cl),
        ],
        out_specs=(
            pl.BlockSpec((height, cols // steps, channels), lambda i: (0, i, 0)),
            whole(br, ba, cf),
            whole(br, ba, cl),
        ),
        scratch_shapes=[pltpu.VMEM((lanes, channels), bf), pltpu.VMEM((groups, lanes), bf)],
        name="back",
    )(feats, amat, probs, slope, codes, table, depth_weight.T, merged, lid_grad)
    return merged, cam_grad, lid_grad


def solution(mesh):
    strips = mesh.shape["strip"]
    n = mesh.shape["branch"] * strips
    placed = (
        P(None, AXES, None),
        P(),
        P(),
        P(AXES, None),
        P(None, AXES, None),
        P(None, AXES),
        P(),
        P(),
        P(None, AXES, None),
    )
    return jax.shard_map(
        functools.partial(local, n, strips),
        mesh=mesh,
        in_specs=placed,
        out_specs=(P(None, AXES, None),) * 3,
        check_vma=False,
    )
```

```python
import functools

import jax
import jax.numpy as jnp
from jax import lax
from jax.experimental import pallas as pl
from jax.experimental.pallas import tpu as pltpu
from jax.sharding import PartitionSpec as P

AXES = ("branch", "strip")
CH = 8
BLOCK = 16


def rolled_sum(low, mid, high, period):
    rows = mid.shape[0]
    place = lax.broadcasted_iota(jnp.int32, mid.shape, 0) & (period - 1)
    down = jnp.where(place == 0, 0.0, pltpu.roll(low, 1, 0))
    up = jnp.where(place == period - 1, 0.0, pltpu.roll(high, rows - 1, 0))
    return mid + down + up


def conv_rows(src, starts, rows, weights, layer, height):
    taps = [
        jnp.concatenate([src[pl.ds(s + i * height, rows), :] for s in starts], axis=0)
        for i in range(3)
    ]
    x = jnp.concatenate(taps, axis=1)
    channels = taps[0].shape[1]
    z = [
        jnp.dot(
            x,
            weights[layer, 3 * dy : 3 * dy + 3].reshape(3 * channels, -1),
            preferred_element_type=jnp.float32,
        )
        for dy in range(3)
    ]
    total = rolled_sum(z[0], z[1], z[2], height)
    return jnp.maximum(total, 0.0).astype(jnp.bfloat16)


def one_hot_rows(rows, sources, source_of):
    p = lax.broadcasted_iota(jnp.int32, (rows, sources), 0)
    q = lax.broadcasted_iota(jnp.int32, (rows, sources), 1)
    return jnp.where(source_of(p) == q, 1.0, 0.0).astype(jnp.bfloat16)


def row_numbers(shape):
    return lax.broadcasted_iota(jnp.int32, shape, 0).astype(jnp.float32).astype(jnp.bfloat16)


def pick_of(row_id, codes, j):
    groups, lanes = row_id.shape
    code = jnp.broadcast_to(codes[pl.ds(j, 1), :], (16, lanes)).astype(jnp.bfloat16)
    code = jnp.concatenate([code] * (groups // 16), axis=0)
    one, zero = jnp.ones((), jnp.bfloat16), jnp.zeros((), jnp.bfloat16)
    return jnp.where(row_id[...] == code, one, zero)


def block_turn():
    shift = BLOCK.bit_length() - 1
    return one_hot_rows(
        BLOCK * BLOCK,
        BLOCK * BLOCK,
        lambda p: ((p & (BLOCK - 1)) << shift) + (p >> shift),
    )


def kernel(
    n, strips, cols, height, br, ba, bins_n,
    img, cw_hbm, wd, bins, pillars, counts, lw, cot, mw_hbm,
    merged_o, lidgrad_o, table, codes, feats_o, amat_o, probs_o, slope_o,
    cw, mw, xin, y1, y2, feats, wdp, probs, slope, sums, low, row_id, amat, parts, sendbuf,
    rp1, rp2, rp3, rm1, rm2, rm3, win, lidwin, cotwin,
    local_sem, out_sem, send_sem, recv_sem,
):
    me = lax.axis_index(AXES[0]) * strips + lax.axis_index(AXES[1])
    ch_rows = CH * height
    lanes = wdp.shape[0]

    def dev(d):
        t = lax.rem(me + d + n, n)
        return (t // strips, t % strips)

    barrier = pltpu.get_barrier_semaphore()
    for d in (1, 2, 3, -1, -2, -3):
        pl.semaphore_signal(
            barrier, inc=1, device_id=dev(d), device_id_type=pl.DeviceIdType.MESH
        )
    layers = cw.shape[0]
    fetches = [
        pltpu.make_async_copy(cw_hbm.at[k], cw.at[k], local_sem.at[k]) for k in range(layers)
    ]
    fetches.append(pltpu.make_async_copy(mw_hbm, mw, local_sem.at[layers]))
    for copy in fetches:
        copy.start()

    turn = block_turn()
    for j0 in range(0, cols, BLOCK):
        for h0 in range(0, height, BLOCK):
            block = img[h0 : h0 + BLOCK, j0 : j0 + BLOCK, :].reshape(BLOCK * BLOCK, -1)
            turned = jnp.dot(turn, block, preferred_element_type=jnp.float32)
            turned = turned.astype(jnp.bfloat16)
            for c in range(BLOCK):
                at = (3 + j0 + c) * height + h0
                xin[pl.ds(at, BLOCK), :] = turned[c * BLOCK : (c + 1) * BLOCK]

    sec = ba * br
    cot_own, lid_own = (ba + 1) * br, (ba + 2) * br
    cot_f = cot[...].astype(jnp.float32)
    for a in range(ba):
        cotwin[pl.ds(cot_own + a * br, br), :] = cot_f[:, a, :].astype(jnp.bfloat16)
    points = counts[...]
    scale = (points > 0).astype(jnp.float32) / jnp.maximum(points, 1).astype(jnp.float32)
    pil = pillars[...].astype(jnp.float32)
    pil = jnp.concatenate(
        [pil[k] * scale[:, k : k + 1] for k in range(2 * br)], axis=0
    ).astype(jnp.bfloat16)
    lb, la = br.bit_length() - 1, ba.bit_length() - 1

    def pillar_row(p):
        r, a, uv = p & (br - 1), (p >> lb) & (ba - 1), p >> (lb + la)
        return ((2 * r + (uv >> 1)) << (la + 1)) + 2 * a + (uv & 1)

    gathered = jnp.dot(
        one_hot_rows(4 * sec, 4 * sec, pillar_row), pil, preferred_element_type=jnp.float32
    ).astype(jnp.bfloat16)
    taps = jnp.concatenate([gathered[k * sec : (k + 1) * sec] for k in range(4)], axis=1)
    lid = jnp.dot(
        taps, lw[...].reshape(taps.shape[1], -1), preferred_element_type=jnp.float32
    )
    lidwin[pl.ds(lid_own, sec), :] = jnp.maximum(lid, 0.0).astype(jnp.bfloat16)

    cell = br * ba
    sh_cell, sh_ba, sh_br = cell.bit_length() - 1, ba.bit_length() - 1, br.bit_length() - 1
    raw = bins[...]
    off = (raw >> sh_cell) - me + 1
    off = jnp.where(off < 0, off + n, off)
    off = jnp.where(off >= n, off - n, off)
    in_cell = raw & (cell - 1)
    code = (((off << sh_ba) + (in_cell & (ba - 1))) << sh_br) + (in_cell >> sh_ba)
    codes[...] = jnp.full(codes.shape, -1.0, jnp.float32)
    codes[:, 0:bins_n] = code.astype(jnp.float32)
    row_id[...] = row_numbers(row_id.shape)
    wdp[...] = jnp.zeros_like(wdp)
    wdp[0:bins_n, :] = wd[...]
    parts[...] = jnp.zeros_like(parts)
    fetches[0].wait()

    def interior(src, dst, layer, first, shift):
        def step(i, carry):
            c = jnp.minimum(first + CH * i, cols - first - CH) + shift
            at = pl.multiple_of(c * height, height)
            dst[pl.ds(at, ch_rows), :] = conv_rows(src, [at], ch_rows, cw, layer, height)
            return carry

        lax.fori_loop(0, cols // CH, step, 0)

    interior(xin, y1, 0, 1, 2)
    pl.semaphore_wait(barrier, 6)

    messages = []

    def send(src, dst, d):
        m = len(messages)
        copy = pltpu.make_async_remote_copy(
            src_ref=src,
            dst_ref=dst,
            send_sem=send_sem.at[m],
            recv_sem=recv_sem.at[m],
            device_id=dev(d),
            device_id_type=pl.DeviceIdType.MESH,
        )
        copy.start()
        messages.append(copy)

    h3 = 3 * height
    send(xin.at[pl.ds(cols * height, h3)], xin.at[pl.ds(0, h3)], 1)
    send(xin.at[pl.ds(h3, h3)], xin.at[pl.ds((cols + 3) * height, h3)], -1)
    for window, start, edge in ((cotwin, cot_own, br), (lidwin, lid_own, 2 * br)):
        mine = window.at[pl.ds(start, sec)]
        send(mine, window.at[pl.ds(edge, sec)], 1)
        send(mine, window.at[pl.ds(start + sec, sec)], -1)
        last = window.at[pl.ds(start + sec - edge, edge)]
        send(last, window.at[pl.ds(0, edge)], 2)
        send(window.at[pl.ds(start, edge)], window.at[pl.ds(start + 2 * sec, edge)], -2)

    fetches[1].wait()
    interior(y1, y2, 1, 2, 1)
    fetches[2].wait()
    interior(y2, feats, 2, 3, 0)

    messages[0].wait_recv()
    messages[1].wait_recv()
    for layer, (src, dst, extra) in enumerate(((xin, y1, 4), (y1, y2, 2), (y2, feats, 0))):
        right = (cols + extra - 3) * height
        edge = conv_rows(src, [0, right], h3, cw, layer, height)
        dst[pl.ds(0, h3), :] = edge[:h3]
        dst[pl.ds(right, h3), :] = edge[h3:]

    outs = []

    def write(src, dst):
        copy = pltpu.make_async_copy(src, dst, out_sem.at[len(outs)])
        copy.start()
        outs.append(copy)

    used = 3 * ba * br
    lane = lax.broadcasted_iota(jnp.int32, (ch_rows, lanes), 1)

    def soften(i, carry):
        at = pl.multiple_of(i * ch_rows, ch_rows)
        f = feats[pl.ds(at, ch_rows), :]
        logits = lax.dot_general(
            f, wdp[...], (((1,), (1,)), ((), ())), preferred_element_type=jnp.float32
        )
        e = jnp.exp(-jnp.abs(logits))
        soft = jnp.maximum(logits, 0.0) + jnp.log1p(e) + 0.05
        soft = jnp.where(lane < bins_n, soft, 0.0)
        inv = 1.0 / jnp.sum(soft, axis=1, keepdims=True)
        p = soft * inv
        probs[pl.ds(at, ch_rows), :] = p
        slope[pl.ds(at, ch_rows), :] = logits
        sums[pl.ds(at, ch_rows), :] = inv
        low[pl.ds(at, ch_rows), :] = p.astype(jnp.bfloat16)
        return carry

    lax.fori_loop(0, cols // CH, soften, 0)

    def lift(i, carry):
        for c in range(CH):
            j = i * CH + c
            at = pl.multiple_of(j * height, height)
            a = lax.dot_general(
                low[pl.ds(at, height), :],
                pick_of(row_id, codes, j),
                (((1,), (1,)), ((), ())),
                preferred_element_type=jnp.float32,
            )
            amat[pl.ds(at, height), :] = a.astype(jnp.bfloat16)
        return carry

    lax.fori_loop(0, cols // CH, lift, 0)

    def gather(i, carry):
        at = pl.multiple_of(i * 2 * ch_rows, 2 * ch_rows)
        parts[...] += lax.dot_general(
            amat[pl.ds(at, 2 * ch_rows), :],
            feats[pl.ds(at, 2 * ch_rows), :],
            (((0,), (0,)), ((), ())),
            preferred_element_type=jnp.float32,
        )
        return carry

    lax.fori_loop(0, cols // (2 * CH), gather, 0)

    mine = parts[0:used, :]
    sendbuf[...] = mine.astype(jnp.bfloat16)
    n1, n2, n3 = (2 * ba + 2) * br, (ba + 2) * br, 2 * br
    send(sendbuf.at[pl.ds(used - n1, n1)], rp1, 1)
    send(sendbuf.at[pl.ds(0, n1)], rm1, -1)
    send(sendbuf.at[pl.ds(used - n2, n2)], rp2, 2)
    send(sendbuf.at[pl.ds(0, n2)], rm2, -2)
    send(sendbuf.at[pl.ds(used - n3, n3)], rp3, 3)
    send(sendbuf.at[pl.ds(0, n3)], rm3, -3)
    write(feats, feats_o)
    write(amat, amat_o)
    write(probs, probs_o)

    def bend(i, carry):
        at = pl.multiple_of(i * ch_rows, ch_rows)
        sig = jax.nn.sigmoid(slope[pl.ds(at, ch_rows), :]) * sums[pl.ds(at, ch_rows), :]
        slope[pl.ds(at, ch_rows), :] = jnp.where(lane < bins_n, sig, 0.0)
        return carry

    lax.fori_loop(0, cols // CH, bend, 0)
    for copy in messages[2:10]:
        copy.wait_recv()
    fetches[layers].wait()
    channels = feats.shape[1]
    total = win.shape[0]
    act_rows = total - 2 * br

    def merge(source, lo, hi):
        x = jnp.concatenate([source[i * br : i * br + act_rows] for i in range(3)], axis=1)
        z = [
            jnp.dot(
                x,
                mw[3 * dy : 3 * dy + 3, lo:hi, :].reshape(3 * (hi - lo), -1),
                preferred_element_type=jnp.float32,
            )
            for dy in range(3)
        ]
        return rolled_sum(z[0], z[1], z[2], br)

    lid_act = merge(lidwin[...], channels, mw.shape[1])
    write(slope, slope_o)
    win[...] = jnp.zeros_like(win)
    win[pl.ds(2 * br, used), :] = mine
    for copy in messages[10:]:
        copy.wait_recv()
    for got, size in ((rp1, n1), (rp2, n2), (rp3, n3)):
        win[pl.ds(0, size), :] += got[...].astype(jnp.float32)
    for got, size in ((rm1, n1), (rm2, n2), (rm3, n3)):
        win[pl.ds(total - size, size), :] += got[...].astype(jnp.float32)

    act = lid_act + merge(win[...].astype(jnp.bfloat16), 0, channels)
    gate = 1.0 / (1.0 + jnp.exp(-act))
    merged = (act * gate)[cot_own : cot_own + sec]
    merged_o[...] = jnp.stack(
        [merged[a * br : (a + 1) * br] for a in range(ba)], axis=1
    ).astype(jnp.bfloat16)
    grad_pre = (
        cotwin[...].astype(jnp.float32) * (gate * (1.0 + act * (1.0 - gate)))
    ).astype(jnp.bfloat16)

    def merge_back(first, rows, lo, hi):
        y = []
        for dy in range(3):
            acc = None
            for i in range(3):
                term = lax.dot_general(
                    grad_pre[first + (2 - i) * br : first + (2 - i) * br + rows],
                    mw[3 * dy + i, lo:hi, :],
                    (((1,), (1,)), ((), ())),
                    preferred_element_type=jnp.float32,
                )
                acc = term if acc is None else acc + term
            y.append(acc)
        return rolled_sum(y[2], y[1], y[0], br)

    table[...] = merge_back(0, used, 0, channels).astype(jnp.bfloat16)
    lid_grad = merge_back(sec, sec, channels, mw.shape[1])
    lidgrad_o[...] = jnp.stack(
        [lid_grad[a * br : (a + 1) * br] for a in range(ba)], axis=1
    ).astype(jnp.bfloat16)
    for copy in messages:
        copy.wait_send()
    for copy in outs:
        copy.wait()


def back_kernel(
    height, bins_n,
    feats, amat, probs, slope, codes, table, wd, merged, lid_grad,
    camgrad_o, merged_o, lidgrad_o,
    wdp, row_id,
):
    step = pl.program_id(0)
    ch_rows = CH * height

    @pl.when(step == 0)
    def _():
        merged_o[...] = merged[...]
        lidgrad_o[...] = lid_grad[...]
        wdp[...] = jnp.zeros_like(wdp)
        wdp[0:bins_n, :] = wd[...]
        row_id[...] = row_numbers(row_id.shape)

    turn = block_turn()
    blocks = []
    chunks = feats.shape[0] // ch_rows
    tab = table[...]
    for k in range(chunks):
        rows = pl.ds(k * ch_rows, ch_rows)
        g = lax.dot_general(
            feats[rows, :], tab, (((1,), (1,)), ((), ())), preferred_element_type=jnp.float32
        ).astype(jnp.bfloat16)
        direct = jnp.dot(amat[rows, :], tab, preferred_element_type=jnp.float32)
        gp = jnp.concatenate(
            [
                jnp.dot(
                    g[c * height : (c + 1) * height],
                    pick_of(row_id, codes, (step * chunks + k) * CH + c),
                    preferred_element_type=jnp.float32,
                )
                for c in range(CH)
            ],
            axis=0,
        )
        mean = jnp.sum(gp * probs[rows, :], axis=1, keepdims=True)
        gl = ((gp - mean) * slope[rows, :]).astype(jnp.bfloat16)
        depth = jnp.dot(gl, wdp[...], preferred_element_type=jnp.float32)
        blocks.append((direct + depth).astype(jnp.bfloat16))
    block = jnp.concatenate(blocks, axis=0)
    for h0 in range(0, height, BLOCK):
        part = jnp.concatenate(
            [block[c * height + h0 : c * height + h0 + BLOCK] for c in range(BLOCK)], axis=0
        )
        turned = jnp.dot(turn, part, preferred_element_type=jnp.float32)
        camgrad_o[h0 : h0 + BLOCK, :, :] = turned.astype(jnp.bfloat16).reshape(
            BLOCK, BLOCK, -1
        )


def local(
    n, strips,
    image_feats, cam_weights, depth_weight, ray_bins, pillar_sums, pillar_counts,
    lidar_weight, merge_weight, out_cotangent,
):
    height, cols, channels = image_feats.shape
    br, ba, cf = out_cotangent.shape
    bins_n = depth_weight.shape[1]
    cl = pillar_sums.shape[2]
    lanes = -(-bins_n // 128) * 128
    used = groups = 3 * ba * br
    total = (3 * ba + 4) * br
    bf, f32 = jnp.bfloat16, jnp.float32

    vm = pl.BlockSpec(memory_space=pltpu.VMEM)
    hbm = pl.BlockSpec(memory_space=pl.ANY)
    n1, n2, n3 = (2 * ba + 2) * br, (ba + 2) * br, 2 * br
    rows = cols * height
    merged, lid_grad, table, codes, feats, amat, probs, slope = pl.pallas_call(
        functools.partial(kernel, n, strips, cols, height, br, ba, bins_n),
        out_shape=(
            jax.ShapeDtypeStruct((br, ba, cf), bf),
            jax.ShapeDtypeStruct((br, ba, cl), bf),
            jax.ShapeDtypeStruct((groups, channels), bf),
            jax.ShapeDtypeStruct((cols, lanes), f32),
            jax.ShapeDtypeStruct((rows, channels), bf),
            jax.ShapeDtypeStruct((rows, groups), bf),
            jax.ShapeDtypeStruct((rows, lanes), f32),
            jax.ShapeDtypeStruct((rows, lanes), f32),
        ),
        in_specs=[vm, hbm, vm, vm, vm, vm, vm, vm, hbm],
        out_specs=(vm,) * 4 + (hbm,) * 4,
        scratch_shapes=[
            pltpu.VMEM(cam_weights.shape, bf),
            pltpu.VMEM(merge_weight.shape, bf),
            pltpu.VMEM(((cols + 6) * height, channels), bf),
            pltpu.VMEM(((cols + 4) * height, channels), bf),
            pltpu.VMEM(((cols + 2) * height, channels), bf),
            pltpu.VMEM((cols * height, channels), bf),
            pltpu.VMEM((lanes, channels), bf),
            pltpu.VMEM((cols * height, lanes), f32),
            pltpu.VMEM((cols * height, lanes), f32),
            pltpu.VMEM((cols * height, 1), f32),
            pltpu.VMEM((cols * height, lanes), bf),
            pltpu.VMEM((groups, lanes), bf),
            pltpu.VMEM((cols * height, groups), bf),
            pltpu.VMEM((groups, channels), f32),
            pltpu.VMEM((used, channels), bf),
            pltpu.VMEM((n1, channels), bf),
            pltpu.VMEM((n2, channels), bf),
            pltpu.VMEM((n3, channels), bf),
            pltpu.VMEM((n1, channels), bf),
            pltpu.VMEM((n2, channels), bf),
            pltpu.VMEM((n3, channels), bf),
            pltpu.VMEM((total, channels), f32),
            pltpu.VMEM((total, cl), bf),
            pltpu.VMEM((total - 2 * br, cf), bf),
            pltpu.SemaphoreType.DMA((cam_weights.shape[0] + 1,)),
            pltpu.SemaphoreType.DMA((4,)),
            pltpu.SemaphoreType.DMA((16,)),
            pltpu.SemaphoreType.DMA((16,)),
        ],
        compiler_params=pltpu.CompilerParams(
            collective_id=0, has_side_effects=True, vmem_limit_bytes=58 * 1024 * 1024
        ),
        name="bev",
    )(
        image_feats, cam_weights, depth_weight.T, ray_bins, pillar_sums, pillar_counts.T,
        lidar_weight, out_cotangent, merge_weight,
    )
    steps = cols // BLOCK

    def rowed(width):
        return pl.BlockSpec((rows // steps, width), lambda i: (i, 0))

    def whole(*shape):
        return pl.BlockSpec(shape, lambda i: (0,) * len(shape))

    cam_grad, merged, lid_grad = pl.pallas_call(
        functools.partial(back_kernel, height, bins_n),
        grid=(steps,),
        out_shape=(
            jax.ShapeDtypeStruct((height, cols, channels), bf),
            jax.ShapeDtypeStruct((br, ba, cf), bf),
            jax.ShapeDtypeStruct((br, ba, cl), bf),
        ),
        in_specs=[
            rowed(channels), rowed(groups), rowed(lanes), rowed(lanes),
            whole(cols, lanes), whole(groups, channels), whole(bins_n, channels),
            whole(br, ba, cf), whole(br, ba, cl),
        ],
        out_specs=(
            pl.BlockSpec((height, cols // steps, channels), lambda i: (0, i, 0)),
            whole(br, ba, cf),
            whole(br, ba, cl),
        ),
        scratch_shapes=[pltpu.VMEM((lanes, channels), bf), pltpu.VMEM((groups, lanes), bf)],
        name="back",
    )(feats, amat, probs, slope, codes, table, depth_weight.T, merged, lid_grad)
    return merged, cam_grad, lid_grad


def solution(mesh):
    strips = mesh.shape["strip"]
    n = mesh.shape["branch"] * strips
    placed = (
        P(None, AXES, None),
        P(),
        P(),
        P(AXES, None),
        P(None, AXES, None),
        P(None, AXES),
        P(),
        P(),
        P(None, AXES, None),
    )
    return jax.shard_map(
        functools.partial(local, n, strips),
        mesh=mesh,
        in_specs=placed,
        out_specs=(P(None, AXES, None),) * 3,
        check_vma=False,
    )
```

```python
import functools

import jax
import jax.numpy as jnp
from jax import lax
from jax.experimental import pallas as pl
from jax.experimental.pallas import tpu as pltpu
from jax.sharding import PartitionSpec as P

AXES = ("branch", "strip")
CH = 8
BLOCK = 16


def rolled_sum(low, mid, high, period):
    rows = mid.shape[0]
    place = lax.broadcasted_iota(jnp.int32, mid.shape, 0) & (period - 1)
    down = jnp.where(place == 0, 0.0, pltpu.roll(low, 1, 0))
    up = jnp.where(place == period - 1, 0.0, pltpu.roll(high, rows - 1, 0))
    return mid + down + up


def conv_rows(src, pieces, weights, layer, height):
    taps = [
        jnp.concatenate([src[pl.ds(s + i * height, rows), :] for s, rows in pieces], axis=0)
        for i in range(3)
    ]
    x = jnp.concatenate(taps, axis=1)
    channels = taps[0].shape[1]
    z = [
        jnp.dot(
            x,
            weights[layer, 3 * dy : 3 * dy + 3].reshape(3 * channels, -1),
            preferred_element_type=jnp.float32,
        )
        for dy in range(3)
    ]
    total = rolled_sum(z[0], z[1], z[2], height)
    return jnp.maximum(total, 0.0).astype(jnp.bfloat16)


def one_hot_rows(rows, sources, source_of):
    p = lax.broadcasted_iota(jnp.int32, (rows, sources), 0)
    q = lax.broadcasted_iota(jnp.int32, (rows, sources), 1)
    return jnp.where(source_of(p) == q, 1.0, 0.0).astype(jnp.bfloat16)


def row_numbers(shape):
    return lax.broadcasted_iota(jnp.int32, shape, 0).astype(jnp.float32).astype(jnp.bfloat16)


def pick_of(row_id, codes, j):
    groups, lanes = row_id.shape
    code = jnp.broadcast_to(codes[pl.ds(j, 1), :], (16, lanes)).astype(jnp.bfloat16)
    code = jnp.concatenate([code] * (groups // 16), axis=0)
    one, zero = jnp.ones((), jnp.bfloat16), jnp.zeros((), jnp.bfloat16)
    return jnp.where(row_id[...] == code, one, zero)


def block_turn():
    shift = BLOCK.bit_length() - 1
    return one_hot_rows(
        BLOCK * BLOCK,
        BLOCK * BLOCK,
        lambda p: ((p & (BLOCK - 1)) << shift) + (p >> shift),
    )


def kernel(
    n, strips, cols, height, br, ba, bins_n,
    img_hbm, cw_hbm, wd, bins, pillars, counts, lw, cot, mw_hbm,
    merged_o, lidgrad_o, table, codes, feats_o, amat_o, probs_o, slope_o,
    img, cw, mw, xin, y1, y2, feats, wdp, probs, slope, sums, low, row_id, amat, parts, sendbuf,
    rp1, rp2, rp3, rm1, rm2, rm3, win, lidwin, cotwin,
    local_sem, out_sem, send_sem, recv_sem,
):
    me = lax.axis_index(AXES[0]) * strips + lax.axis_index(AXES[1])
    ch_rows = CH * height
    lanes = wdp.shape[0]

    def dev(d):
        t = lax.rem(me + d + n, n)
        return (t // strips, t % strips)

    barrier = pltpu.get_barrier_semaphore()
    for d in (1, 2, 3, -1, -2, -3):
        pl.semaphore_signal(
            barrier, inc=1, device_id=dev(d), device_id_type=pl.DeviceIdType.MESH
        )
    layers = cw.shape[0]
    image = pltpu.make_async_copy(img_hbm, img, local_sem.at[layers + 1])
    image.start()
    fetches = [
        pltpu.make_async_copy(cw_hbm.at[k], cw.at[k], local_sem.at[k]) for k in range(layers)
    ]
    fetches.append(pltpu.make_async_copy(mw_hbm, mw, local_sem.at[layers]))
    for copy in fetches:
        copy.start()

    sec = ba * br
    cot_own, lid_own = (ba + 1) * br, (ba + 2) * br
    cot_f = cot[...].astype(jnp.float32)
    for a in range(ba):
        cotwin[pl.ds(cot_own + a * br, br), :] = cot_f[:, a, :].astype(jnp.bfloat16)
    points = counts[...]
    scale = (points > 0).astype(jnp.float32) / jnp.maximum(points, 1).astype(jnp.float32)
    pil = pillars[...].astype(jnp.float32)
    pil = jnp.concatenate(
        [pil[k] * scale[:, k : k + 1] for k in range(2 * br)], axis=0
    ).astype(jnp.bfloat16)
    lb, la = br.bit_length() - 1, ba.bit_length() - 1

    def pillar_row(p):
        r, a, uv = p & (br - 1), (p >> lb) & (ba - 1), p >> (lb + la)
        return ((2 * r + (uv >> 1)) << (la + 1)) + 2 * a + (uv & 1)

    gathered = jnp.dot(
        one_hot_rows(4 * sec, 4 * sec, pillar_row), pil, preferred_element_type=jnp.float32
    ).astype(jnp.bfloat16)
    taps = jnp.concatenate([gathered[k * sec : (k + 1) * sec] for k in range(4)], axis=1)
    lid = jnp.dot(
        taps, lw[...].reshape(taps.shape[1], -1), preferred_element_type=jnp.float32
    )
    lidwin[pl.ds(lid_own, sec), :] = jnp.maximum(lid, 0.0).astype(jnp.bfloat16)

    cell = br * ba
    sh_cell, sh_ba, sh_br = cell.bit_length() - 1, ba.bit_length() - 1, br.bit_length() - 1
    raw = bins[...]
    off = (raw >> sh_cell) - me + 1
    off = jnp.where(off < 0, off + n, off)
    off = jnp.where(off >= n, off - n, off)
    in_cell = raw & (cell - 1)
    code = (((off << sh_ba) + (in_cell & (ba - 1))) << sh_br) + (in_cell >> sh_ba)
    codes[...] = jnp.full(codes.shape, -1.0, jnp.float32)
    codes[:, 0:bins_n] = code.astype(jnp.float32)
    row_id[...] = row_numbers(row_id.shape)
    wdp[...] = jnp.zeros_like(wdp)
    wdp[0:bins_n, :] = wd[...]
    parts[...] = jnp.zeros_like(parts)
    image.wait()
    turn = block_turn()
    for j0 in range(0, cols, BLOCK):
        for h0 in range(0, height, BLOCK):
            block = img[h0 : h0 + BLOCK, j0 : j0 + BLOCK, :].reshape(BLOCK * BLOCK, -1)
            turned = jnp.dot(turn, block, preferred_element_type=jnp.float32)
            turned = turned.astype(jnp.bfloat16)
            for c in range(BLOCK):
                at = (3 + j0 + c) * height + h0
                xin[pl.ds(at, BLOCK), :] = turned[c * BLOCK : (c + 1) * BLOCK]
    fetches[0].wait()

    def interior(src, dst, layer, first, shift, count):
        def step(i, carry):
            c = jnp.minimum(first + CH * i, cols - first - CH) + shift
            at = pl.multiple_of(c * height, height)
            dst[pl.ds(at, ch_rows), :] = conv_rows(src, [(at, ch_rows)], cw, layer, height)
            return carry

        lax.fori_loop(0, count, step, 0)

    full = cols // CH
    interior(xin, y1, 0, 1, 2, full)
    pl.semaphore_wait(barrier, 6)

    messages = []

    def send(src, dst, d):
        m = len(messages)
        copy = pltpu.make_async_remote_copy(
            src_ref=src,
            dst_ref=dst,
            send_sem=send_sem.at[m],
            recv_sem=recv_sem.at[m],
            device_id=dev(d),
            device_id_type=pl.DeviceIdType.MESH,
        )
        copy.start()
        messages.append(copy)

    h3 = 3 * height
    send(xin.at[pl.ds(cols * height, h3)], xin.at[pl.ds(0, h3)], 1)
    send(xin.at[pl.ds(h3, h3)], xin.at[pl.ds((cols + 3) * height, h3)], -1)
    for window, start, edge in ((cotwin, cot_own, br), (lidwin, lid_own, 2 * br)):
        mine = window.at[pl.ds(start, sec)]
        send(mine, window.at[pl.ds(edge, sec)], 1)
        send(mine, window.at[pl.ds(start + sec, sec)], -1)
        last = window.at[pl.ds(start + sec - edge, edge)]
        send(last, window.at[pl.ds(0, edge)], 2)
        send(window.at[pl.ds(start, edge)], window.at[pl.ds(start + 2 * sec, edge)], -2)

    fetches[1].wait()
    interior(y1, y2, 1, 2, 1, full - 1)
    fetches[2].wait()
    interior(y2, feats, 2, 3, 0, full - 2)

    messages[0].wait_recv()
    messages[1].wait_recv()
    for layer, (src, dst, extra, done) in enumerate(
        ((xin, y1, 4, cols - 2), (y1, y2, 2, cols - CH), (y2, feats, 0, cols - 2 * CH))
    ):
        right = (3 + done) * height
        size = (cols + extra) * height - right
        edge = conv_rows(src, [(0, h3), (right, size)], cw, layer, height)
        dst[pl.ds(0, h3), :] = edge[:h3]
        dst[pl.ds(right, size), :] = edge[h3:]

    outs = []

    def write(src, dst):
        copy = pltpu.make_async_copy(src, dst, out_sem.at[len(outs)])
        copy.start()
        outs.append(copy)

    used = 3 * ba * br
    lane = lax.broadcasted_iota(jnp.int32, (ch_rows, lanes), 1)

    def soften(i, carry):
        at = pl.multiple_of(i * ch_rows, ch_rows)
        f = feats[pl.ds(at, ch_rows), :]
        logits = lax.dot_general(
            f, wdp[...], (((1,), (1,)), ((), ())), preferred_element_type=jnp.float32
        )
        e = jnp.exp(-jnp.abs(logits))
        soft = jnp.maximum(logits, 0.0) + jnp.log1p(e) + 0.05
        soft = jnp.where(lane < bins_n, soft, 0.0)
        inv = 1.0 / jnp.sum(soft, axis=1, keepdims=True)
        p = soft * inv
        probs[pl.ds(at, ch_rows), :] = p
        slope[pl.ds(at, ch_rows), :] = logits
        sums[pl.ds(at, ch_rows), :] = inv
        low[pl.ds(at, ch_rows), :] = p.astype(jnp.bfloat16)
        return carry

    lax.fori_loop(0, cols // CH, soften, 0)

    def lift(i, carry):
        for c in range(CH):
            j = i * CH + c
            at = pl.multiple_of(j * height, height)
            a = lax.dot_general(
                low[pl.ds(at, height), :],
                pick_of(row_id, codes, j),
                (((1,), (1,)), ((), ())),
                preferred_element_type=jnp.float32,
            )
            amat[pl.ds(at, height), :] = a.astype(jnp.bfloat16)
        return carry

    lax.fori_loop(0, cols // CH, lift, 0)

    def gather(i, carry):
        at = pl.multiple_of(i * 2 * ch_rows, 2 * ch_rows)
        parts[...] += lax.dot_general(
            amat[pl.ds(at, 2 * ch_rows), :],
            feats[pl.ds(at, 2 * ch_rows), :],
            (((0,), (0,)), ((), ())),
            preferred_element_type=jnp.float32,
        )
        return carry

    lax.fori_loop(0, cols // (2 * CH), gather, 0)

    mine = parts[0:used, :]
    sendbuf[...] = mine.astype(jnp.bfloat16)
    n1, n2, n3 = (2 * ba + 2) * br, (ba + 2) * br, 2 * br
    send(sendbuf.at[pl.ds(used - n1, n1)], rp1, 1)
    send(sendbuf.at[pl.ds(0, n1)], rm1, -1)
    send(sendbuf.at[pl.ds(used - n2, n2)], rp2, 2)
    send(sendbuf.at[pl.ds(0, n2)], rm2, -2)
    send(sendbuf.at[pl.ds(used - n3, n3)], rp3, 3)
    send(sendbuf.at[pl.ds(0, n3)], rm3, -3)
    write(feats, feats_o)
    write(amat, amat_o)
    write(probs, probs_o)

    def bend(i, carry):
        at = pl.multiple_of(i * ch_rows, ch_rows)
        sig = jax.nn.sigmoid(slope[pl.ds(at, ch_rows), :]) * sums[pl.ds(at, ch_rows), :]
        slope[pl.ds(at, ch_rows), :] = jnp.where(lane < bins_n, sig, 0.0)
        return carry

    lax.fori_loop(0, cols // CH, bend, 0)
    for copy in messages[2:10]:
        copy.wait_recv()
    fetches[layers].wait()
    channels = feats.shape[1]
    total = win.shape[0]
    act_rows = total - 2 * br

    def merge(source, lo, hi):
        x = jnp.concatenate([source[i * br : i * br + act_rows] for i in range(3)], axis=1)
        z = [
            jnp.dot(
                x,
                mw[3 * dy : 3 * dy + 3, lo:hi, :].reshape(3 * (hi - lo), -1),
                preferred_element_type=jnp.float32,
            )
            for dy in range(3)
        ]
        return rolled_sum(z[0], z[1], z[2], br)

    lid_act = merge(lidwin[...], channels, mw.shape[1])
    write(slope, slope_o)
    win[...] = jnp.zeros_like(win)
    win[pl.ds(2 * br, used), :] = mine
    for copy in messages[10:]:
        copy.wait_recv()
    for got, size in ((rp1, n1), (rp2, n2), (rp3, n3)):
        win[pl.ds(0, size), :] += got[...].astype(jnp.float32)
    for got, size in ((rm1, n1), (rm2, n2), (rm3, n3)):
        win[pl.ds(total - size, size), :] += got[...].astype(jnp.float32)

    act = lid_act + merge(win[...].astype(jnp.bfloat16), 0, channels)
    gate = 1.0 / (1.0 + jnp.exp(-act))
    merged = (act * gate)[cot_own : cot_own + sec]
    merged_o[...] = jnp.stack(
        [merged[a * br : (a + 1) * br] for a in range(ba)], axis=1
    ).astype(jnp.bfloat16)
    grad_pre = (
        cotwin[...].astype(jnp.float32) * (gate * (1.0 + act * (1.0 - gate)))
    ).astype(jnp.bfloat16)

    def merge_back(first, rows, lo, hi):
        y = []
        for dy in range(3):
            acc = None
            for i in range(3):
                term = lax.dot_general(
                    grad_pre[first + (2 - i) * br : first + (2 - i) * br + rows],
                    mw[3 * dy + i, lo:hi, :],
                    (((1,), (1,)), ((), ())),
                    preferred_element_type=jnp.float32,
                )
                acc = term if acc is None else acc + term
            y.append(acc)
        return rolled_sum(y[2], y[1], y[0], br)

    table[...] = merge_back(0, used, 0, channels).astype(jnp.bfloat16)
    lid_grad = merge_back(sec, sec, channels, mw.shape[1])
    lidgrad_o[...] = jnp.stack(
        [lid_grad[a * br : (a + 1) * br] for a in range(ba)], axis=1
    ).astype(jnp.bfloat16)
    for copy in messages:
        copy.wait_send()
    for copy in outs:
        copy.wait()


def back_kernel(
    height, bins_n,
    feats, amat, probs, slope, codes, table, wd, merged, lid_grad,
    camgrad_o, merged_o, lidgrad_o,
    wdp, row_id,
):
    step = pl.program_id(0)
    ch_rows = CH * height

    @pl.when(step == 0)
    def _():
        merged_o[...] = merged[...]
        lidgrad_o[...] = lid_grad[...]
        wdp[...] = jnp.zeros_like(wdp)
        wdp[0:bins_n, :] = wd[...]
        row_id[...] = row_numbers(row_id.shape)

    turn = block_turn()
    blocks = []
    chunks = feats.shape[0] // ch_rows
    tab = table[...]
    for k in range(chunks):
        rows = pl.ds(k * ch_rows, ch_rows)
        g = lax.dot_general(
            feats[rows, :], tab, (((1,), (1,)), ((), ())), preferred_element_type=jnp.float32
        ).astype(jnp.bfloat16)
        direct = jnp.dot(amat[rows, :], tab, preferred_element_type=jnp.float32)
        gp = jnp.concatenate(
            [
                jnp.dot(
                    g[c * height : (c + 1) * height],
                    pick_of(row_id, codes, (step * chunks + k) * CH + c),
                    preferred_element_type=jnp.float32,
                )
                for c in range(CH)
            ],
            axis=0,
        )
        mean = jnp.sum(gp * probs[rows, :], axis=1, keepdims=True)
        gl = ((gp - mean) * slope[rows, :]).astype(jnp.bfloat16)
        depth = jnp.dot(gl, wdp[...], preferred_element_type=jnp.float32)
        blocks.append((direct + depth).astype(jnp.bfloat16))
    block = jnp.concatenate(blocks, axis=0)
    for h0 in range(0, height, BLOCK):
        part = jnp.concatenate(
            [block[c * height + h0 : c * height + h0 + BLOCK] for c in range(BLOCK)], axis=0
        )
        turned = jnp.dot(turn, part, preferred_element_type=jnp.float32)
        camgrad_o[h0 : h0 + BLOCK, :, :] = turned.astype(jnp.bfloat16).reshape(
            BLOCK, BLOCK, -1
        )


def local(
    n, strips,
    image_feats, cam_weights, depth_weight, ray_bins, pillar_sums, pillar_counts,
    lidar_weight, merge_weight, out_cotangent,
):
    height, cols, channels = image_feats.shape
    br, ba, cf = out_cotangent.shape
    bins_n = depth_weight.shape[1]
    cl = pillar_sums.shape[2]
    lanes = -(-bins_n // 128) * 128
    used = groups = 3 * ba * br
    total = (3 * ba + 4) * br
    bf, f32 = jnp.bfloat16, jnp.float32

    vm = pl.BlockSpec(memory_space=pltpu.VMEM)
    hbm = pl.BlockSpec(memory_space=pl.ANY)
    n1, n2, n3 = (2 * ba + 2) * br, (ba + 2) * br, 2 * br
    rows = cols * height
    merged, lid_grad, table, codes, feats, amat, probs, slope = pl.pallas_call(
        functools.partial(kernel, n, strips, cols, height, br, ba, bins_n),
        out_shape=(
            jax.ShapeDtypeStruct((br, ba, cf), bf),
            jax.ShapeDtypeStruct((br, ba, cl), bf),
            jax.ShapeDtypeStruct((groups, channels), bf),
            jax.ShapeDtypeStruct((cols, lanes), f32),
            jax.ShapeDtypeStruct((rows, channels), bf),
            jax.ShapeDtypeStruct((rows, groups), bf),
            jax.ShapeDtypeStruct((rows, lanes), f32),
            jax.ShapeDtypeStruct((rows, lanes), f32),
        ),
        in_specs=[hbm, hbm, vm, vm, vm, vm, vm, vm, hbm],
        out_specs=(vm,) * 4 + (hbm,) * 4,
        scratch_shapes=[
            pltpu.VMEM(image_feats.shape, bf),
            pltpu.VMEM(cam_weights.shape, bf),
            pltpu.VMEM(merge_weight.shape, bf),
            pltpu.VMEM(((cols + 6) * height, channels), bf),
            pltpu.VMEM(((cols + 4) * height, channels), bf),
            pltpu.VMEM(((cols + 2) * height, channels), bf),
            pltpu.VMEM((cols * height, channels), bf),
            pltpu.VMEM((lanes, channels), bf),
            pltpu.VMEM((cols * height, lanes), f32),
            pltpu.VMEM((cols * height, lanes), f32),
            pltpu.VMEM((cols * height, 1), f32),
            pltpu.VMEM((cols * height, lanes), bf),
            pltpu.VMEM((groups, lanes), bf),
            pltpu.VMEM((cols * height, groups), bf),
            pltpu.VMEM((groups, channels), f32),
            pltpu.VMEM((used, channels), bf),
            pltpu.VMEM((n1, channels), bf),
            pltpu.VMEM((n2, channels), bf),
            pltpu.VMEM((n3, channels), bf),
            pltpu.VMEM((n1, channels), bf),
            pltpu.VMEM((n2, channels), bf),
            pltpu.VMEM((n3, channels), bf),
            pltpu.VMEM((total, channels), f32),
            pltpu.VMEM((total, cl), bf),
            pltpu.VMEM((total - 2 * br, cf), bf),
            pltpu.SemaphoreType.DMA((cam_weights.shape[0] + 2,)),
            pltpu.SemaphoreType.DMA((4,)),
            pltpu.SemaphoreType.DMA((16,)),
            pltpu.SemaphoreType.DMA((16,)),
        ],
        compiler_params=pltpu.CompilerParams(
            collective_id=0, has_side_effects=True, vmem_limit_bytes=58 * 1024 * 1024
        ),
        name="bev",
    )(
        image_feats, cam_weights, depth_weight.T, ray_bins, pillar_sums, pillar_counts.T,
        lidar_weight, out_cotangent, merge_weight,
    )
    steps = cols // BLOCK

    def rowed(width):
        return pl.BlockSpec((rows // steps, width), lambda i: (i, 0))

    def whole(*shape):
        return pl.BlockSpec(shape, lambda i: (0,) * len(shape))

    cam_grad, merged, lid_grad = pl.pallas_call(
        functools.partial(back_kernel, height, bins_n),
        grid=(steps,),
        out_shape=(
            jax.ShapeDtypeStruct((height, cols, channels), bf),
            jax.ShapeDtypeStruct((br, ba, cf), bf),
            jax.ShapeDtypeStruct((br, ba, cl), bf),
        ),
        in_specs=[
            rowed(channels), rowed(groups), rowed(lanes), rowed(lanes),
            whole(cols, lanes), whole(groups, channels), whole(bins_n, channels),
            whole(br, ba, cf), whole(br, ba, cl),
        ],
        out_specs=(
            pl.BlockSpec((height, cols // steps, channels), lambda i: (0, i, 0)),
            whole(br, ba, cf),
            whole(br, ba, cl),
        ),
        scratch_shapes=[pltpu.VMEM((lanes, channels), bf), pltpu.VMEM((groups, lanes), bf)],
        name="back",
    )(feats, amat, probs, slope, codes, table, depth_weight.T, merged, lid_grad)
    return merged, cam_grad, lid_grad


def solution(mesh):
    strips = mesh.shape["strip"]
    n = mesh.shape["branch"] * strips
    placed = (
        P(None, AXES, None),
        P(),
        P(),
        P(AXES, None),
        P(None, AXES, None),
        P(None, AXES),
        P(),
        P(),
        P(None, AXES, None),
    )
    return jax.shard_map(
        functools.partial(local, n, strips),
        mesh=mesh,
        in_specs=placed,
        out_specs=(P(None, AXES, None),) * 3,
        check_vma=False,
    )
```
